512 devices in a mesh: grp: 32 (over x, y, z_hi), tile: 16 (over z_lo, core).
Axes of the slice: x: 4, y: 4, z: 16 (z_hi: 2, z_lo: 8; z = z_hi * 8 + z_lo), core: 2. Of those that a mesh axis runs over, the one named last changes fastest.
Arguments:
- log_cond: float32 [32, 128, 32, 128], P('grp', 'tile'), may hold values from -3 to 3
- potential: float32 [32, 128, 32, 128], P('grp', 'tile'), may hold values from -6 to 6
- noise: float32 [2, 32, 128, 32, 128], P(None, 'grp', 'tile'), may hold values from -3 to 3
- source: float32 [128, 32, 128], P('tile'), may hold values from -6 to 6
- parents: int32 [32], replicated, may hold values from 0 to 31
- accept: int32 [2, 32], P(None, 'grp'), may hold values 0 or 1
- weights: float32 [32], P('grp'), may hold values from 0.1 to 10
Outputs:
- conduct_out: float32 [32, 128, 32, 128], P('grp', 'tile')
- potential_out: float32 [32, 128, 32, 128], P('grp', 'tile')
- moments: float32 [1024, 1024], P('tile')
The draws below stay inside these ranges and needn't reach their ends.
Inputs may be any that keep to these rules, and one draw needn't show every extreme that they name: `parents`: parent indices of offspring.
All inputs are finite; a program needn't handle non-finite values. No bound on the sum of `accept` on one device may be relied on, other than what follows from the above.
Results may differ from the reference program's by a relative error of at most 0.0001.
Values sent between devices are 32-bit elements; how exact they have to be, the bound alone decides.
A program may use at most 64 MiB of HBM per device.

```python
import math
import jax
import jax.numpy as jnp
import numpy as np
from jax import lax

CX = 8
NY = 32
NZ = 128
MOVES = 2
P_SIZE = 32
NX = 128
COEF = 1024
N_TILE = 16


def with_ends(result, own_key, low, high):
    place = [jax.random.randint(jax.random.fold_in(own_key, axis), (), 0, length) for axis, length in enumerate(result.shape)]
    longest = result.shape.index(max(result.shape))
    next_to = place[:longest] + [(place[longest] + 1) % result.shape[longest]] + place[longest + 1:]
    return result.at[tuple(place)].set(low).at[tuple(next_to)].set(high)


def levels(key, extent, split, low, largest):
    def one(position, parts):
        draws = jax.random.uniform(jax.random.fold_in(jax.random.fold_in(key, 6), position), (parts,), jnp.float32, low / len(split), largest / len(split))
        return jnp.repeat(jnp.exp(draws), extent[position] // parts).reshape((-1,) + (1,) * (len(extent) - position - 1))

    gain = one(*split[0])
    for cut in split[1:]:
        gain = gain * one(*cut)
    return gain


def rank_bounds(amount, slope):
    weights = [(1 << 20) // math.isqrt(rank ** slope) + 1 for rank in range(1, amount + 1)]
    deviation = 1 + sum(weights) // (1 << 30)
    return np.cumsum(np.array([max(1, weight // deviation) for weight in weights]))


def ranked_ids(stream_key, extent, number_of, slope):
    table = rank_bounds(number_of, slope)
    pick = jax.random.randint(jax.random.fold_in(stream_key, 1), extent, 0, int(table[number_of - 1]))
    grade = jnp.searchsorted(jnp.asarray(table, jnp.int32), pick, side="right")
    return jax.random.permutation(jax.random.fold_in(stream_key, 2), number_of)[grade].astype(jnp.int32)


def bell_draw(own_key, shape, scale, most, shards=(), dtype=jnp.bfloat16):
    level = levels(own_key, shape, shards, -0.22, 0.18) if shards else 1.0
    values = jax.random.normal(own_key, shape, jnp.float32) * scale * level
    return jnp.minimum(jnp.maximum(values, -most), most).astype(dtype)


def setup_inputs(seed: int = 0) -> dict:
    seeds = jax.random.split(jax.random.key(seed), 8)
    log_cond = bell_draw(seeds[0], (P_SIZE, NX, NY, NZ), 0.5, 3.0, ((0, 32), (1, 16)), jnp.float32)
    potential = bell_draw(seeds[1], (P_SIZE, NX, NY, NZ), 1.0, 6.0, ((0, 32), (1, 16)), jnp.float32)
    noise = bell_draw(seeds[2], (MOVES, P_SIZE, NX, NY, NZ), 0.5, 3.0, ((1, 32), (2, 16)), jnp.float32)
    source = bell_draw(seeds[3], (NX, NY, NZ), 1.0, 6.0, ((0, 16),), jnp.float32)
    parents = with_ends(ranked_ids(seeds[4], (P_SIZE,), P_SIZE, 2), jax.random.fold_in(seeds[4], 3), 0, P_SIZE - 1).astype(jnp.int32)
    accept = with_ends((jax.random.randint(seeds[5], (MOVES, P_SIZE), 0, 2) < 1).astype(jnp.int32), jax.random.fold_in(seeds[5], 1), 0, 1)
    weights = jnp.clip(jnp.exp(math.log(10.0) - 4.6051702 * jax.random.uniform(seeds[6], (P_SIZE,), jnp.float32) ** levels(seeds[6], (P_SIZE,), ((0, 32),), -0.2, 0.2)), 0.1, 10.0)
    return dict(log_cond=log_cond, potential=potential, noise=noise, source=source, parents=parents, accept=accept, weights=weights)


prior_keep = 0.8
prior_fresh = 0.6
relax_weight = 0.8


def neighbours(padded):
    return [padded[2:, 1:-1, 1:-1], padded[:-2, 1:-1, 1:-1],
            padded[1:-1, 2:, 1:-1], padded[1:-1, :-2, 1:-1],
            padded[1:-1, 1:-1, 2:], padded[1:-1, 1:-1, :-2]]


def relax_sweep(cond_ext, pot_ext, source):
    cond_pad = jnp.pad(cond_ext, ((0, 0), (1, 1), (1, 1)))
    pot_pad = jnp.pad(pot_ext, ((0, 0), (1, 1), (1, 1)))
    conductivity = jnp.exp(cond_pad)
    centre_k = conductivity[1:-1, 1:-1, 1:-1]
    centre = pot_pad[1:-1, 1:-1, 1:-1]
    flux_sum = jnp.zeros_like(centre)
    coef_sum = jnp.zeros_like(centre)
    for near_k, near_v in zip(neighbours(conductivity), neighbours(pot_pad)):
        face = 0.5 * (centre_k + near_k)
        flux_sum = flux_sum + face * near_v
        coef_sum = coef_sum + face
    return (1.0 - relax_weight) * centre + relax_weight * (source + flux_sum) / coef_sum


def pad_first(field):
    return jnp.pad(field, ((1, 1), (0, 0), (0, 0)))


def reference(log_cond, potential, noise, source, parents, accept, weights):
    conduct = log_cond[parents]
    pot = potential[parents]
    sweep_all = jax.vmap(lambda cond_now, pot_now: relax_sweep(pad_first(cond_now), pad_first(pot_now), source))
    for move_index in range(MOVES):
        proposal = prior_keep * conduct + prior_fresh * noise[move_index]
        relaxed_once = sweep_all(proposal, pot)
        relaxed_twice = sweep_all(proposal, relaxed_once)
        accepted = (accept[move_index] > 0)[:, None, None, None]
        conduct = jnp.where(accepted, proposal, conduct)
        pot = jnp.where(accepted, relaxed_twice, pot)
    weight_sum = jnp.sum(weights)

    def accumulate(running, element):
        field, share = element
        blocks = field.reshape(N_TILE, CX, NY, NZ)
        moment_one = jnp.einsum('txyz,tuyw->xzuw', blocks, blocks,
                                precision=lax.Precision.HIGHEST).reshape(COEF, COEF)
        return running + share * moment_one, None

    moments, _ = lax.scan(accumulate, jnp.zeros((COEF, COEF), jnp.float32), (pot, weights / weight_sum))
    return conduct, pot, moments
```

```python
import jax
import jax.numpy as jnp
from jax import lax
from jax.experimental import pallas as pl
from jax.experimental.pallas import tpu as pltpu
from jax.sharding import PartitionSpec as P

MESH = pl.DeviceIdType.MESH
F32 = jnp.float32
BF16 = jnp.bfloat16
CHUNKS = 2
HALO = 4


def device(x, y, z, core):
    return {"grp": (x * 4 + y) * 2 + z // 8, "tile": (z % 8) * 2 + core}


def split(value):
    high = value.astype(BF16)
    return high, (value - high.astype(F32)).astype(BF16)


def shifted(value, axis, fill):
    size = value.shape[axis]
    place = lax.broadcasted_iota(jnp.int32, value.shape, axis)
    up = jnp.where(place == 0, fill, pltpu.roll(value, 1, axis))
    down = jnp.where(place == size - 1, fill, pltpu.roll(value, size - 1, axis))
    return up + down


def kernel(
    log_cond, potential, noise, source, parents, accept, weights,
    cond_out, pot_out, mom_out,
    gathered, sent, picked, zsent, zgot, halo, field, prop, kcon, inv, once,
    perm, rows, cols, partial, corner, summed, zsum, wbuf,
    send_gather, recv_gather, send_pick, recv_pick, send_z, recv_z, send_halo, recv_halo,
    send_rows, recv_rows, send_core, recv_core, send_sum, recv_sum, send_all, recv_all, send_w, recv_w,
):
    group, tile = lax.axis_index("grp"), lax.axis_index("tile")
    x, y, z = group // 8, (group // 2) % 4, (group % 2) * 8 + tile // 2
    high_z, core = group % 2, tile % 2
    pending = {}

    def copy(src, dst, sends, recvs, target):
        made = pltpu.make_async_remote_copy(
            src_ref=src, dst_ref=dst, send_sem=sends, recv_sem=recvs, device_id=target, device_id_type=MESH
        )
        made.start()
        pending[id(made)] = made
        return made

    def drain(copies):
        for made in copies:
            made.wait_send()
            del pending[id(made)]

    def along(axis, d):
        if axis == 0:
            return device((x + d) % 4, y, z, core)
        return device(x, (y + d) % 4, z, core)

    beyond = device(x, y, (z + 15 + 2 * core) % 16, 1 - core)
    partner = device(x, y, z, 1 - core)
    below = {"grp": (x * 4 + y) * 2 + ((z * 2 + core + 31) % 32) // 16, "tile": (tile + 15) % 16}
    above = {"grp": (x * 4 + y) * 2 + ((z * 2 + core + 1) % 32) // 16, "tile": (tile + 1) % 16}

    barrier = pltpu.get_barrier_semaphore()
    greeted = [device((x + a) % 4, (y + b) % 4, z, core) for a in range(4) for b in range(4) if a or b]
    greeted += [device(x, y, (z + d) % 16, core) for d in range(1, 16)]
    greeted += [beyond, partner]
    for other in greeted:
        pl.semaphore_signal(barrier, inc=1, device_id=other, device_id_type=MESH)
    pl.semaphore_wait(barrier, len(greeted))

    fields = (log_cond, potential)
    planes = 8 // CHUNKS
    chunk = [pl.ds(k * planes, planes) for k in range(CHUNKS)]
    gathers = {}
    for k in range(CHUNKS):
        for f in range(2):
            for d in range(1, 4):
                at = (f * CHUNKS + k) * 3 + d - 1
                gathers[f, k, d] = copy(
                    fields[f].at[chunk[k]], gathered[f][k].at[d], send_gather.at[at], recv_gather.at[at], along(f, d)
                )

    halos = []
    parts = ((noise.at[0], 0, 4), (noise.at[1], 4, 2), (source, 6, 3))
    for i, (ref, start, width) in enumerate(parts):
        halos.append(copy(ref.at[pl.ds(0, width)], halo.at[1, pl.ds(start, width)], send_halo.at[i], recv_halo.at[i], below))
        halos.append(
            copy(ref.at[pl.ds(8 - width, width)], halo.at[0, pl.ds(start, width)], send_halo.at[3 + i], recv_halo.at[3 + i], above)
        )
    for f in range(2):
        for k in range(CHUNKS):
            gathered[f][k][0] = fields[f][chunk[k]]

    wvec = jnp.full((8, 128), weights[0], F32)
    wbuf[0, 0] = wvec
    wcopies = [copy(wbuf.at[0, 0], wbuf.at[0, d], send_w.at[d - 1], recv_w.at[d - 1], along(0, d)) for d in range(1, 4)]

    def parent(a, b, c):
        return parents[(a * 4 + b) * 2 + c]

    def coordinate(p, axis):
        return p // 8 if axis == 0 else (p // 2) % 4

    mine = (x, y)
    picks = {}

    def spread(f, k, kind):
        first, second = f, 1 - f
        to_z = high_z if kind == 0 else 1 - high_z
        for d in (1, 2, 3, 0):
            p = parent((x + d) % 4, y, to_z) if second == 0 else parent(x, (y + d) % 4, to_z)
            slot = (mine[first] - coordinate(p, first) + 4) % 4
            block = gathered[f][k][slot]
            if d == 0:
                picked[f][kind][k][0] = block
            else:
                sent[f, kind, d - 1, chunk[k]] = block
                at = ((f * 2 + kind) * CHUNKS + k) * 3 + d - 1
                picks[f, kind, k, d] = copy(
                    sent.at[f, kind, d - 1, chunk[k]], picked[f][kind][k].at[d], send_pick.at[at], recv_pick.at[at], along(second, d)
                )

    def choose(f, k, kind):
        second = 1 - f
        for d in range(1, 4):
            picks[f, kind, k, d].wait_recv()
        p = parent(x, y, high_z if kind == 0 else 1 - high_z)
        return picked[f][kind][k][(mine[second] - coordinate(p, second) + 4) % 4]

    for k in range(CHUNKS):
        for f in range(2):
            for d in range(1, 4):
                gathers[f, k, d].wait_recv()
            spread(f, k, 1)
    zcopies = {}
    for k in range(CHUNKS):
        for f in range(2):
            zsent[f, chunk[k]] = choose(f, k, 1)
            at = f * CHUNKS + k
            zcopies[f, k] = copy(
                zsent.at[f, chunk[k]], zgot.at[f, chunk[k]], send_z.at[at], recv_z.at[at], device(x, y, (z + 8) % 16, core)
            )
    for k in range(CHUNKS):
        for f in range(2):
            spread(f, k, 0)

    for c in wcopies:
        c.wait_recv()
    wbuf[1, 0] = wbuf[0, 0] + wbuf[0, 1] + wbuf[0, 2] + wbuf[0, 3]
    wcopies = [copy(wbuf.at[1, 0], wbuf.at[1, d], send_w.at[2 + d], recv_w.at[2 + d], along(1, d)) for d in range(1, 4)]

    from_here = jnp.full((1, 32, 128), (parent(x, y, high_z) % 2 == high_z).astype(jnp.int32)) > 0
    interior = pl.ds(HALO, 8)
    for k in range(CHUNKS):
        for f in range(2):
            own = choose(f, k, 0)
            zcopies[f, k].wait_recv()
            field[f, pl.ds(HALO + k * planes, planes)] = jnp.where(from_here, own, zgot[f, chunk[k]])

    edges = []
    for f in range(2):
        edges.append(
            copy(field.at[f, pl.ds(HALO, HALO)], field.at[f, pl.ds(HALO + 8, HALO)], send_halo.at[6 + f], recv_halo.at[6 + f], below)
        )
        edges.append(copy(field.at[f, pl.ds(8, HALO)], field.at[f, pl.ds(0, HALO)], send_halo.at[8 + f], recv_halo.at[8 + f], above))

    for c in wcopies:
        c.wait_recv()
    wbuf[2, 0] = wbuf[1, 0] + wbuf[1, 1] + wbuf[1, 2] + wbuf[1, 3]
    wlast = copy(wbuf.at[2, 0], wbuf.at[2, 1], send_w.at[6], recv_w.at[6], device(x, y, (z + 8) % 16, core))

    for c in halos + edges:
        c.wait_recv()

    has_below = jnp.full((32, 128), (tile > 0).astype(jnp.int32))
    has_above = jnp.full((32, 128), (tile < 15).astype(jnp.int32))

    def inside(i, value):
        if i < HALO:
            return jnp.where(has_below > 0, value, 0.0)
        if i >= HALO + 8:
            return jnp.where(has_above > 0, value, 0.0)
        return value

    for f in range(2):
        for i in (*range(HALO), *range(HALO + 8, 2 * HALO + 8)):
            field[f, i] = inside(i, field[f, i])

    def border(ref, start, width, i):
        if i < HALO:
            return halo[0, start + width - HALO + i]
        if i >= HALO + 8:
            return halo[1, start + i - HALO - 8]
        return ref[i - HALO]

    def sweep(i, v_at):
        here, low, up = v_at(i), v_at(i - 1), v_at(i + 1)
        k = kcon[i]
        kv = k * here
        near = low + up + shifted(here, 0, 0.0) + shifted(here, 1, 0.0)
        weighted = kcon[i - 1] * low + kcon[i + 1] * up + shifted(kv, 0, 0.0) + shifted(kv, 1, 0.0)
        return k, near, weighted, here

    for m in range(2):
        edge = 2 * m
        last = 2 * HALO + 8 - edge
        for i in range(edge, last):
            fresh = border(noise.at[m], 0 if m == 0 else 4, 4 if m == 0 else 2, i)
            value = inside(i, 0.8 * field[0, i] + 0.6 * fresh)
            prop[i] = value
            kcon[i] = jnp.exp(value)
        flag = jnp.full((32, 128), accept[m, 0]) > 0
        for i in range(edge + 1, last - 1):
            k, near, weighted, here = sweep(i, lambda j: field[1, j])
            inv[i] = 0.8 / (6.0 * k + kcon[i - 1] + kcon[i + 1] + shifted(k, 0, 1.0) + shifted(k, 1, 1.0))
            value = 0.2 * here + (2.0 * border(source, 6, 3, i) + k * near + weighted) * inv[i]
            once[i] = inside(i, value)
        if m == 0:
            drain(edges)
        for i in range(edge + 2, last - 2):
            k, near, weighted, here = sweep(i, lambda j: once[j])
            value = 0.2 * here + (2.0 * border(source, 6, 3, i) + k * near + weighted) * inv[i]
            field[0, i] = jnp.where(flag, prop[i], field[0, i])
            field[1, i] = jnp.where(flag, inside(i, value), field[1, i])

    final = field[1, interior]
    cond_out[...] = field[0, interior]
    pot_out[...] = final

    columns = [
        copy(field.at[1, pl.ds(HALO + 2 * ((y + d) % 4), 2)], cols.at[0, d], send_rows.at[d - 1], recv_rows.at[d - 1], along(1, d))
        for d in range(1, 4)
    ]
    cols[0, 0] = field[1, pl.ds(HALO + 2 * y, 2)]
    scaled = final * weights[0]
    into = lax.broadcasted_iota(jnp.int32, (512, 512), 0)
    out = lax.broadcasted_iota(jnp.int32, (512, 512), 1)
    wanted = ((out // 16) % 4) * 128 + ((out // 64) % 2) * 64 + (out // 128) * 16 + out % 16
    select = jnp.where(into == wanted, 1.0, 0.0).astype(BF16)
    stacked = jnp.concatenate(
        [jnp.concatenate([scaled[4 * half + j] for j in range(4)], axis=1) for half in range(2)], axis=0
    )
    high, low = split(stacked)
    shuffled = jnp.dot(high, select, preferred_element_type=F32) + jnp.dot(low, select, preferred_element_type=F32)
    for j in range(4):
        for half in range(2):
            perm[j, half] = shuffled[32 * half : 32 * half + 32, 128 * j : 128 * j + 128]
    taken = [
        copy(perm.at[(x + d) % 4], rows.at[0, d], send_rows.at[2 + d], recv_rows.at[2 + d], along(0, d)) for d in range(1, 4)
    ]
    rows[0, 0] = perm[x]
    for c in columns:
        c.wait_recv()
    columns = [copy(cols.at[0], cols.at[d], send_rows.at[5 + d], recv_rows.at[5 + d], along(0, d)) for d in range(1, 4)]
    for c in taken:
        c.wait_recv()
    taken = [copy(rows.at[0], rows.at[d], send_rows.at[8 + d], recv_rows.at[8 + d], along(1, d)) for d in range(1, 4)]
    for c in columns + taken:
        c.wait_recv()

    right = jnp.concatenate(
        [jnp.concatenate([cols[dx, dy, 0], cols[dx, dy, 1]], axis=1) for dy in range(4) for dx in range(4)], axis=0
    )
    right_high, right_low = split(right)
    for half in range(2):
        left = jnp.concatenate([rows[dy, dx, half] for dy in range(4) for dx in range(4)], axis=0).T
        left_high, left_low = split(left)
        product = (
            jnp.dot(left_high, right_high, preferred_element_type=F32)
            + jnp.dot(left_high, right_low, preferred_element_type=F32)
            + jnp.dot(left_low, right_high, preferred_element_type=F32)
        )
        for c in range(2):
            partial[c, half] = product[64 * c : 64 * c + 64]
    swapped = copy(partial.at[1 - core], corner, send_core, recv_core, partner)
    swapped.wait_recv()
    for half in range(2):
        total = partial[core, half] + corner[half]
        for j in range(4):
            summed[4 * half + j] = total[16 * j : 16 * j + 16]
    sums = [
        copy(summed.at[(z + d) % 8], zsum.at[d], send_sum.at[d], recv_sum.at[d], device(x, y, (z + d) % 16, core))
        for d in range(1, 16)
    ]
    wlast.wait_recv()
    for c in sums:
        c.wait_recv()
    total = summed[z % 8]
    for d in range(1, 16):
        total = total + zsum[d]
    weight_sum = wbuf[2, 0] + wbuf[2, 1]
    mom_out[x, y] = total / weight_sum[0:1, 0:1]
    others = [(a, b) for a in range(4) for b in range(4) if a or b]
    last = [
        copy(
            mom_out.at[x, y], mom_out.at[x, y], send_all.at[i], recv_all.at[i], device((x + a) % 4, (y + b) % 4, z, core)
        )
        for i, (a, b) in enumerate(others)
    ]
    for c in last:
        c.wait_recv()
    for c in pending.values():
        c.wait_send()


def local(log_cond, potential, noise, source, parents, accept, weights):
    vmem, smem = pl.BlockSpec(memory_space=pltpu.VMEM), pl.BlockSpec(memory_space=pltpu.SMEM)
    dma = pltpu.SemaphoreType.DMA
    block = (8, 32, 128)
    four = (4, 8 // CHUNKS, 32, 128)
    wide = (2 * HALO + 8, 32, 128)
    conduct, pot, moments = pl.pallas_call(
        kernel,
        out_shape=(
            jax.ShapeDtypeStruct(block, F32),
            jax.ShapeDtypeStruct(block, F32),
            jax.ShapeDtypeStruct((4, 4, 16, 256), F32),
        ),
        in_specs=[vmem, vmem, vmem, vmem, smem, smem, smem],
        out_specs=(vmem, vmem, vmem),
        scratch_shapes=[
            ((pltpu.VMEM(four, F32),) * CHUNKS,) * 2,
            pltpu.VMEM((2, 2, 3, *block), F32),
            (((pltpu.VMEM(four, F32),) * CHUNKS,) * 2,) * 2,
            pltpu.VMEM((2, *block), F32),
            pltpu.VMEM((2, *block), F32),
            pltpu.VMEM((2, 9, 32, 128), F32),
            pltpu.VMEM((2, *wide), F32),
            pltpu.VMEM(wide, F32),
            pltpu.VMEM(wide, F32),
            pltpu.VMEM(wide, F32),
            pltpu.VMEM(wide, F32),
            pltpu.VMEM((4, 2, 32, 128), F32),
            pltpu.VMEM((4, 4, 2, 32, 128), F32),
            pltpu.VMEM((4, 4, 2, 32, 128), F32),
            pltpu.VMEM((2, 2, 64, 256), F32),
            pltpu.VMEM((2, 64, 256), F32),
            pltpu.VMEM((8, 16, 256), F32),
            pltpu.VMEM((16, 16, 256), F32),
            pltpu.VMEM((3, 4, 8, 128), F32),
            dma((6 * CHUNKS,)), dma((6 * CHUNKS,)),
            dma((12 * CHUNKS,)), dma((12 * CHUNKS,)),
            dma((2 * CHUNKS,)), dma((2 * CHUNKS,)),
            dma((10,)), dma((10,)),
            dma((12,)), dma((12,)),
            dma, dma,
            dma((16,)), dma((16,)),
            dma((15,)), dma((15,)),
            dma((7,)), dma((7,)),
        ],
        compiler_params=pltpu.CompilerParams(collective_id=0, has_side_effects=True),
        name="resample_move",
    )(log_cond[0], potential[0], noise[:, 0], source, parents, accept, weights)
    return conduct[None], pot[None], moments.transpose(0, 2, 1, 3).reshape(64, 1024)


def solution(mesh):
    placed = (
        P("grp", "tile", None, None),
        P("grp", "tile", None, None),
        P(None, "grp", "tile", None, None),
        P("tile", None, None),
        P(),
        P(None, "grp"),
        P("grp"),
    )
    return jax.shard_map(
        local,
        mesh=mesh,
        in_specs=placed,
        out_specs=(P("grp", "tile", None, None), P("grp", "tile", None, None), P("tile", None)),
        check_vma=False,
    )
```

```python
import jax
import jax.numpy as jnp
from jax import lax
from jax.experimental import pallas as pl
from jax.experimental.pallas import tpu as pltpu
from jax.sharding import PartitionSpec as P

MESH = pl.DeviceIdType.MESH
F32 = jnp.float32
BF16 = jnp.bfloat16
CHUNKS = 4
HALO = 4


def device(x, y, z, core):
    return {"grp": (x * 4 + y) * 2 + z // 8, "tile": (z % 8) * 2 + core}


def split(value):
    high = value.astype(BF16)
    return high, (value - high.astype(F32)).astype(BF16)


def shifted(value, axis, fill):
    size = value.shape[axis]
    place = lax.broadcasted_iota(jnp.int32, value.shape, axis)
    up = jnp.where(place == 0, fill, pltpu.roll(value, 1, axis))
    down = jnp.where(place == size - 1, fill, pltpu.roll(value, size - 1, axis))
    return up + down


def kernel(
    log_cond, potential, noise, source, parents, accept, weights,
    cond_out, pot_out, mom_out,
    pot_got, cond_got, sent, picked, zsent, zgot, halo, field, prop, kcon, inv, once,
    perm, rows, cols, partial, corner, summed, zsum, wbuf,
    send_gather, recv_gather, send_pick, recv_pick, send_z, recv_z, send_halo, recv_halo, send_edge, recv_edge,
    send_rows, recv_rows, send_core, recv_core, send_sum, recv_sum, send_all, recv_all, send_w, recv_w,
):
    group, tile = lax.axis_index("grp"), lax.axis_index("tile")
    x, y, z = group // 8, (group // 2) % 4, (group % 2) * 8 + tile // 2
    high_z, core = group % 2, tile % 2
    pending = {}

    def copy(src, dst, sends, recvs, target):
        made = pltpu.make_async_remote_copy(
            src_ref=src, dst_ref=dst, send_sem=sends, recv_sem=recvs, device_id=target, device_id_type=MESH
        )
        made.start()
        pending[id(made)] = made
        return made

    def drain(copies):
        for made in copies:
            made.wait_send()
            del pending[id(made)]

    def along(axis, d):
        if axis == 0:
            return device((x + d) % 4, y, z, core)
        return device(x, (y + d) % 4, z, core)

    beyond = device(x, y, (z + 15 + 2 * core) % 16, 1 - core)
    partner = device(x, y, z, 1 - core)
    below = {"grp": (x * 4 + y) * 2 + ((z * 2 + core + 31) % 32) // 16, "tile": (tile + 15) % 16}
    above = {"grp": (x * 4 + y) * 2 + ((z * 2 + core + 1) % 32) // 16, "tile": (tile + 1) % 16}

    barrier = pltpu.get_barrier_semaphore()
    greeted = [device((x + a) % 4, (y + b) % 4, z, core) for a in range(4) for b in range(4) if a or b]
    greeted += [device(x, y, (z + d) % 16, core) for d in range(1, 16)]
    greeted += [beyond, partner]
    for other in greeted:
        pl.semaphore_signal(barrier, inc=1, device_id=other, device_id_type=MESH)
    pl.semaphore_wait(barrier, len(greeted))

    across = device(x, y, (z + 8) % 16, core)
    planes = 8 // CHUNKS
    chunk = [pl.ds(k * planes, planes) for k in range(CHUNKS)]
    chunks = range(CHUNKS)
    zcond = [
        copy(log_cond.at[chunk[k]], cond_got[k].at[4], send_z.at[k], recv_z.at[k], across) for k in chunks
    ]

    def gather(src, dst, k, kind):
        made = []
        for d in range(1, 4):
            at = (kind * CHUNKS + k) * 3 + d - 1
            made.append(copy(src, dst(d), send_gather.at[at], recv_gather.at[at], along(0, d)))
        return made

    pot_near = [gather(potential.at[chunk[k]], lambda d: pot_got[k].at[d], k, 0) for k in chunks]

    halos = []
    parts = ((noise.at[0], 0, 4), (noise.at[1], 4, 2), (source, 6, 3))
    for i, (ref, start, width) in enumerate(parts):
        halos.append(copy(ref.at[pl.ds(0, width)], halo.at[1, pl.ds(start, width)], send_halo.at[i], recv_halo.at[i], below))
        halos.append(
            copy(ref.at[pl.ds(8 - width, width)], halo.at[0, pl.ds(start, width)], send_halo.at[3 + i], recv_halo.at[3 + i], above)
        )
    cond_near = [gather(log_cond.at[chunk[k]], lambda d: cond_got[k].at[d], k, 1) for k in chunks]
    for k in chunks:
        pot_got[k][0] = potential[chunk[k]]
        cond_got[k][0] = log_cond[chunk[k]]

    wvec = jnp.full((8, 128), weights[0], F32)
    wbuf[0, 0] = wvec
    wcopies = [copy(wbuf.at[0, 0], wbuf.at[0, d], send_w.at[d - 1], recv_w.at[d - 1], along(0, d)) for d in range(1, 4)]

    def parent(a, b, c):
        return parents[(a * 4 + b) * 2 + c]

    picks = {}

    def spread(k, kind):
        to_z = 1 - high_z if kind == 1 else high_z
        for d in (2, 1, 3, 0):
            p = parent(x, (y + d) % 4, to_z)
            slot = (x - p // 8 + 4) % 4
            if kind == 2:
                block = cond_got[k][((p + high_z) % 2) * 4 + slot]
            else:
                block = pot_got[k][slot]
            if d == 0:
                picked[kind][k][0] = block
            else:
                sent[kind, k, d - 1] = block
                at = (kind * CHUNKS + k) * 3 + d - 1
                picks[kind, k, d] = copy(
                    sent.at[kind, k, d - 1], picked[kind][k].at[d], send_pick.at[at], recv_pick.at[at], along(1, d)
                )

    def choose(k, kind):
        for d in range(1, 4):
            picks[kind, k, d].wait_recv()
        p = parent(x, y, 1 - high_z if kind == 1 else high_z)
        return picked[kind][k][(y - (p // 2) % 4 + 4) % 4]

    for k in chunks:
        for c in pot_near[k]:
            c.wait_recv()
        spread(k, 1)
    zpot = []
    for k in chunks:
        zsent[k] = choose(k, 1)
        zpot.append(copy(zsent.at[k], zgot.at[k], send_z.at[CHUNKS + k], recv_z.at[CHUNKS + k], across))
    for k in chunks:
        spread(k, 0)
    cond_far = []
    for k in chunks:
        zcond[k].wait_recv()
        cond_far.append(gather(cond_got[k].at[4], lambda d: cond_got[k].at[4 + d], k, 2))

    for c in wcopies:
        c.wait_recv()
    wbuf[1, 0] = wbuf[0, 0] + wbuf[0, 1] + wbuf[0, 2] + wbuf[0, 3]
    wcopies = [copy(wbuf.at[1, 0], wbuf.at[1, d], send_w.at[2 + d], recv_w.at[2 + d], along(1, d)) for d in range(1, 4)]

    for k in chunks:
        for c in cond_near[k] + cond_far[k]:
            c.wait_recv()
        spread(k, 2)

    from_here = jnp.full((1, 32, 128), (parent(x, y, high_z) % 2 == high_z).astype(jnp.int32)) > 0
    interior = pl.ds(HALO, 8)
    edges = []

    def place(f, k, value):
        start = k * planes
        field[f, pl.ds(HALO + start, planes)] = value
        src, at = field.at[f, pl.ds(HALO + start, planes)], f * CHUNKS + k
        if start < HALO:
            edges.append(copy(src, field.at[f, pl.ds(HALO + 8 + start, planes)], send_edge.at[at], recv_edge.at[at], below))
        else:
            edges.append(copy(src, field.at[f, pl.ds(start - HALO, planes)], send_edge.at[at], recv_edge.at[at], above))

    for k in chunks:
        place(0, k, choose(k, 2))
    for k in chunks:
        own = choose(k, 0)
        zpot[k].wait_recv()
        place(1, k, jnp.where(from_here, own, zgot[k]))

    for c in wcopies:
        c.wait_recv()
    wbuf[2, 0] = wbuf[1, 0] + wbuf[1, 1] + wbuf[1, 2] + wbuf[1, 3]
    wlast = copy(wbuf.at[2, 0], wbuf.at[2, 1], send_w.at[6], recv_w.at[6], across)

    for c in halos + edges:
        c.wait_recv()

    has_below = jnp.full((32, 128), (tile > 0).astype(jnp.int32))
    has_above = jnp.full((32, 128), (tile < 15).astype(jnp.int32))

    def inside(i, value):
        if i < HALO:
            return jnp.where(has_below > 0, value, 0.0)
        if i >= HALO + 8:
            return jnp.where(has_above > 0, value, 0.0)
        return value

    for f in range(2):
        for i in (*range(HALO), *range(HALO + 8, 2 * HALO + 8)):
            field[f, i] = inside(i, field[f, i])

    def border(ref, start, width, i):
        if i < HALO:
            return halo[0, start + width - HALO + i]
        if i >= HALO + 8:
            return halo[1, start + i - HALO - 8]
        return ref[i - HALO]

    def sweep(i, v_at):
        here, low, up = v_at(i), v_at(i - 1), v_at(i + 1)
        k = kcon[i]
        kv = k * here
        near = low + up + shifted(here, 0, 0.0) + shifted(here, 1, 0.0)
        weighted = kcon[i - 1] * low + kcon[i + 1] * up + shifted(kv, 0, 0.0) + shifted(kv, 1, 0.0)
        return k, near, weighted, here

    for m in range(2):
        edge = 2 * m
        last = 2 * HALO + 8 - edge
        for i in range(edge, last):
            fresh = border(noise.at[m], 0 if m == 0 else 4, 4 if m == 0 else 2, i)
            value = inside(i, 0.8 * field[0, i] + 0.6 * fresh)
            prop[i] = value
            kcon[i] = jnp.exp(value)
        flag = jnp.full((32, 128), accept[m]) > 0
        for i in range(edge + 1, last - 1):
            k, near, weighted, here = sweep(i, lambda j: field[1, j])
            inv[i] = 0.8 / (6.0 * k + kcon[i - 1] + kcon[i + 1] + shifted(k, 0, 1.0) + shifted(k, 1, 1.0))
            value = 0.2 * here + (2.0 * border(source, 6, 3, i) + k * near + weighted) * inv[i]
            once[i] = inside(i, value)
        if m == 0:
            drain(edges)
        for i in range(edge + 2, last - 2):
            k, near, weighted, here = sweep(i, lambda j: once[j])
            value = 0.2 * here + (2.0 * border(source, 6, 3, i) + k * near + weighted) * inv[i]
            field[0, i] = jnp.where(flag, prop[i], field[0, i])
            field[1, i] = jnp.where(flag, inside(i, value), field[1, i])

    final = field[1, interior]
    cond_out[...] = field[0, interior]
    pot_out[...] = final

    columns = [
        copy(field.at[1, pl.ds(HALO + 2 * ((y + d) % 4), 2)], cols.at[0, d], send_rows.at[d - 1], recv_rows.at[d - 1], along(1, d))
        for d in range(1, 4)
    ]
    cols[0, 0] = field[1, pl.ds(HALO + 2 * y, 2)]
    scaled = final * weights[0]
    into = lax.broadcasted_iota(jnp.int32, (512, 512), 0)
    out = lax.broadcasted_iota(jnp.int32, (512, 512), 1)
    wanted = ((out // 16) % 4) * 128 + ((out // 64) % 2) * 64 + (out // 128) * 16 + out % 16
    select = jnp.where(into == wanted, 1.0, 0.0).astype(BF16)
    stacked = jnp.concatenate(
        [jnp.concatenate([scaled[4 * half + j] for j in range(4)], axis=1) for half in range(2)], axis=0
    )
    high, low = split(stacked)
    shuffled = jnp.dot(high, select, preferred_element_type=F32) + jnp.dot(low, select, preferred_element_type=F32)
    for j in range(4):
        for half in range(2):
            perm[j, half] = shuffled[32 * half : 32 * half + 32, 128 * j : 128 * j + 128]
    taken = [
        copy(perm.at[(x + d) % 4], rows.at[0, d], send_rows.at[2 + d], recv_rows.at[2 + d], along(0, d)) for d in range(1, 4)
    ]
    rows[0, 0] = perm[x]
    for c in columns:
        c.wait_recv()
    columns = [copy(cols.at[0], cols.at[d], send_rows.at[5 + d], recv_rows.at[5 + d], along(0, d)) for d in range(1, 4)]
    for c in taken:
        c.wait_recv()
    taken = [copy(rows.at[0], rows.at[d], send_rows.at[8 + d], recv_rows.at[8 + d], along(1, d)) for d in range(1, 4)]
    for c in columns + taken:
        c.wait_recv()

    right = jnp.concatenate(
        [jnp.concatenate([cols[dx, dy, 0], cols[dx, dy, 1]], axis=1) for dy in range(4) for dx in range(4)], axis=0
    )
    right_high, right_low = split(right)
    for half in range(2):
        left = jnp.concatenate([rows[dy, dx, half] for dy in range(4) for dx in range(4)], axis=0).T
        left_high, left_low = split(left)
        product = (
            jnp.dot(left_high, right_high, preferred_element_type=F32)
            + jnp.dot(left_high, right_low, preferred_element_type=F32)
            + jnp.dot(left_low, right_high, preferred_element_type=F32)
        )
        for c in range(2):
            partial[c, half] = product[64 * c : 64 * c + 64]
    swapped = copy(partial.at[1 - core], corner, send_core, recv_core, partner)
    swapped.wait_recv()
    for half in range(2):
        total = partial[core, half] + corner[half]
        for j in range(4):
            summed[4 * half + j] = total[16 * j : 16 * j + 16]
    sums = [
        copy(summed.at[(z + d) % 8], zsum.at[d], send_sum.at[d], recv_sum.at[d], device(x, y, (z + d) % 16, core))
        for d in sorted(range(1, 16), key=lambda d: -min(d, 16 - d))
    ]
    wlast.wait_recv()
    for c in sums:
        c.wait_recv()
    total = summed[z % 8]
    for d in range(1, 16):
        total = total + zsum[d]
    weight_sum = wbuf[2, 0] + wbuf[2, 1]
    piece = mom_out.at[pl.ds(pl.multiple_of(x * 16, 16), 16), pl.ds(pl.multiple_of(y * 256, 256), 256)]
    piece[...] = total / weight_sum[0:1, 0:1]
    others = [(a, b) for a in range(4) for b in range(4) if a or b]
    last = [
        copy(
            piece, piece, send_all.at[i], recv_all.at[i], device((x + a) % 4, (y + b) % 4, z, core)
        )
        for i, (a, b) in enumerate(others)
    ]
    for c in last:
        c.wait_recv()
    for c in pending.values():
        c.wait_send()


def local(log_cond, potential, noise, source, parents, accept, weights):
    vmem, smem = pl.BlockSpec(memory_space=pltpu.VMEM), pl.BlockSpec(memory_space=pltpu.SMEM)
    dma = pltpu.SemaphoreType.DMA
    block = (8, 32, 128)
    part = (8 // CHUNKS, 32, 128)
    wide = (2 * HALO + 8, 32, 128)
    conduct, pot, moments = pl.pallas_call(
        kernel,
        out_shape=(
            jax.ShapeDtypeStruct(block, F32),
            jax.ShapeDtypeStruct(block, F32),
            jax.ShapeDtypeStruct((64, 1024), F32),
        ),
        in_specs=[vmem, vmem, vmem, vmem, smem, smem, smem],
        out_specs=(vmem, vmem, vmem),
        scratch_shapes=[
            (pltpu.VMEM((4, *part), F32),) * CHUNKS,
            (pltpu.VMEM((8, *part), F32),) * CHUNKS,
            pltpu.VMEM((3, CHUNKS, 3, *part), F32),
            ((pltpu.VMEM((4, *part), F32),) * CHUNKS,) * 3,
            pltpu.VMEM((CHUNKS, *part), F32),
            pltpu.VMEM((CHUNKS, *part), F32),
            pltpu.VMEM((2, 9, 32, 128), F32),
            pltpu.VMEM((2, *wide), F32),
            pltpu.VMEM(wide, F32),
            pltpu.VMEM(wide, F32),
            pltpu.VMEM(wide, F32),
            pltpu.VMEM(wide, F32),
            pltpu.VMEM((4, 2, 32, 128), F32),
            pltpu.VMEM((4, 4, 2, 32, 128), F32),
            pltpu.VMEM((4, 4, 2, 32, 128), F32),
            pltpu.VMEM((2, 2, 64, 256), F32),
            pltpu.VMEM((2, 64, 256), F32),
            pltpu.VMEM((8, 16, 256), F32),
            pltpu.VMEM((16, 16, 256), F32),
            pltpu.VMEM((3, 4, 8, 128), F32),
            dma((9 * CHUNKS,)), dma((9 * CHUNKS,)),
            dma((9 * CHUNKS,)), dma((9 * CHUNKS,)),
            dma((2 * CHUNKS,)), dma((2 * CHUNKS,)),
            dma((6,)), dma((6,)),
            dma((2 * CHUNKS,)), dma((2 * CHUNKS,)),
            dma((12,)), dma((12,)),
            dma, dma,
            dma((16,)), dma((16,)),
            dma((15,)), dma((15,)),
            dma((7,)), dma((7,)),
        ],
        compiler_params=pltpu.CompilerParams(collective_id=0, has_side_effects=True),
        name="resample_move",
    )(log_cond[0], potential[0], noise[:, 0], source, parents, accept.reshape(-1), weights)
    return conduct[None], pot[None], moments


def solution(mesh):
    placed = (
        P("grp", "tile", None, None),
        P("grp", "tile", None, None),
        P(None, "grp", "tile", None, None),
        P("tile", None, None),
        P(),
        P(None, "grp"),
        P("grp"),
    )
    return jax.shard_map(
        local,
        mesh=mesh,
        in_specs=placed,
        out_specs=(P("grp", "tile", None, None), P("grp", "tile", None, None), P("tile", None)),
        check_vma=False,
    )
```

```python
import jax
import jax.numpy as jnp
from jax import lax
from jax.experimental import pallas as pl
from jax.experimental.pallas import tpu as pltpu
from jax.sharding import PartitionSpec as P

MESH = pl.DeviceIdType.MESH
F32 = jnp.float32
BF16 = jnp.bfloat16
CHUNKS = 4
HALO = 4


def device(x, y, z, core):
    return {"grp": (x * 4 + y) * 2 + z // 8, "tile": (z % 8) * 2 + core}


def split(value):
    high = value.astype(BF16)
    return high, (value - high.astype(F32)).astype(BF16)


def shifted(value, axis, fill):
    size = value.shape[axis]
    place = lax.broadcasted_iota(jnp.int32, value.shape, axis)
    up = jnp.where(place == 0, fill, pltpu.roll(value, 1, axis))
    down = jnp.where(place == size - 1, fill, pltpu.roll(value, size - 1, axis))
    return up + down


def kernel(
    log_cond, potential, noise_in, source_in, parents, accept, weights,
    cond_out, pot_out, mom_out,
    pot_got, cond_got, sent, picked, zsent, zgot, halo, field, prop, kcon, inv, once,
    noise, source, perm, rows, cols, partial, corner, summed, zsum, wbuf,
    send_sem, recv_gather, recv_pick, recv_z, recv_rows, recv_sem, local_sem,
):
    group, tile = lax.axis_index("grp"), lax.axis_index("tile")
    x, y, z = group // 8, (group // 2) % 4, (group % 2) * 8 + tile // 2
    high_z, core = group % 2, tile % 2
    def copy(src, dst, sends, recvs, target):
        pltpu.make_async_remote_copy(
            src_ref=src, dst_ref=dst, send_sem=sends, recv_sem=recvs, device_id=target, device_id_type=MESH
        ).start()

    def arrived(like, sem):
        pltpu.make_async_copy(like, like, sem).wait()

    def along(axis, d):
        if axis == 0:
            return device((x + d) % 4, y, z, core)
        return device(x, (y + d) % 4, z, core)

    beyond = device(x, y, (z + 15 + 2 * core) % 16, 1 - core)
    partner = device(x, y, z, 1 - core)
    below = {"grp": (x * 4 + y) * 2 + ((z * 2 + core + 31) % 32) // 16, "tile": (tile + 15) % 16}
    above = {"grp": (x * 4 + y) * 2 + ((z * 2 + core + 1) % 32) // 16, "tile": (tile + 1) % 16}

    planes = 8 // CHUNKS
    chunk = [pl.ds(k * planes, planes) for k in range(CHUNKS)]
    chunks = range(CHUNKS)
    loads = [pltpu.make_async_copy(noise_in, noise, local_sem.at[0]), pltpu.make_async_copy(source_in, source, local_sem.at[0])]
    for k in chunks:
        loads.append(pltpu.make_async_copy(potential.at[chunk[k]], pot_got[k].at[0], local_sem.at[1]))
        loads.append(pltpu.make_async_copy(log_cond.at[chunk[k]], cond_got[k].at[0], local_sem.at[2]))

    barrier = pltpu.get_barrier_semaphore()
    greeted = [device((x + a) % 4, (y + b) % 4, z, core) for a in range(4) for b in range(4) if a or b]
    greeted += [device(x, y, (z + d) % 16, core) for d in range(1, 16)]
    greeted += [beyond, partner]
    for other in greeted:
        pl.semaphore_signal(barrier, inc=1, device_id=other, device_id_type=MESH)
    for c in loads:
        c.start()
    pl.semaphore_wait(barrier, len(greeted))

    across = device(x, y, (z + 8) % 16, core)
    for k in chunks:
        copy(log_cond.at[chunk[k]], cond_got[k].at[4], send_sem.at[2], recv_z.at[0, k], across)

    def gather(src, got, first, k, kind):
        for d in range(1, 4):
            copy(src, got.at[first + d], send_sem.at[0], recv_gather.at[kind, k], along(0, d))

    for k in chunks:
        gather(potential.at[chunk[k]], pot_got[k], 0, k, 0)

    for ref, start, width in ((noise_in.at[0], 0, 4), (noise_in.at[1], 4, 2), (source_in, 6, 3)):
        copy(ref.at[pl.ds(0, width)], halo.at[1, pl.ds(start, width)], send_sem.at[3], recv_sem.at[0], below)
        copy(ref.at[pl.ds(8 - width, width)], halo.at[0, pl.ds(start, width)], send_sem.at[3], recv_sem.at[0], above)
    for k in chunks:
        gather(log_cond.at[chunk[k]], cond_got[k], 0, k, 1)

    wbuf[0, 0] = jnp.full((8, 128), weights[0], F32)
    for d in range(1, 4):
        copy(wbuf.at[0, 0], wbuf.at[0, d], send_sem.at[5], recv_sem.at[2], along(0, d))

    def parent(a, b, c):
        return parents[(a * 4 + b) * 2 + c]

    def spread(k, kind):
        to_z = 1 - high_z if kind == 1 else high_z
        for d in (2, 1, 3, 0):
            p = parent(x, (y + d) % 4, to_z)
            slot = (x - p // 8 + 4) % 4
            if kind == 2:
                block = cond_got[k][((p + high_z) % 2) * 4 + slot]
            else:
                block = pot_got[k][slot]
            if d == 0:
                picked[kind][k][0] = block
            else:
                sent[kind, k, d - 1] = block
                copy(sent.at[kind, k, d - 1], picked[kind][k].at[d], send_sem.at[1], recv_pick.at[kind, k], along(1, d))

    def choose(k, kind):
        arrived(picked[kind][k].at[pl.ds(1, 3)], recv_pick.at[kind, k])
        p = parent(x, y, 1 - high_z if kind == 1 else high_z)
        return picked[kind][k][(y - (p // 2) % 4 + 4) % 4]

    arrived(sent.at[0], local_sem.at[0])
    arrived(noise.at[0], local_sem.at[1])
    arrived(noise.at[0], local_sem.at[2])
    for k in chunks:
        arrived(pot_got[k].at[pl.ds(1, 3)], recv_gather.at[0, k])
        spread(k, 1)
    for k in chunks:
        zsent[k] = choose(k, 1)
        copy(zsent.at[k], zgot.at[k], send_sem.at[2], recv_z.at[1, k], across)
    for k in chunks:
        spread(k, 0)
    for k in chunks:
        arrived(cond_got[k].at[4], recv_z.at[0, k])
        gather(cond_got[k].at[4], cond_got[k], 4, k, 2)

    arrived(wbuf.at[0, pl.ds(1, 3)], recv_sem.at[2])
    wbuf[1, 0] = wbuf[0, 0] + wbuf[0, 1] + wbuf[0, 2] + wbuf[0, 3]
    for d in range(1, 4):
        copy(wbuf.at[1, 0], wbuf.at[1, d], send_sem.at[6], recv_sem.at[3], along(1, d))

    for k in chunks:
        arrived(cond_got[k].at[pl.ds(1, 3)], recv_gather.at[1, k])
        arrived(cond_got[k].at[pl.ds(5, 3)], recv_gather.at[2, k])
        spread(k, 2)

    from_here = jnp.full((1, 32, 128), (parent(x, y, high_z) % 2 == high_z).astype(jnp.int32)) > 0
    interior = pl.ds(HALO, 8)

    def place(f, k, value):
        start = k * planes
        field[f, pl.ds(HALO + start, planes)] = value
        src = field.at[f, pl.ds(HALO + start, planes)]
        if start < HALO:
            copy(src, field.at[f, pl.ds(HALO + 8 + start, planes)], send_sem.at[4], recv_sem.at[1], below)
        else:
            copy(src, field.at[f, pl.ds(start - HALO, planes)], send_sem.at[4], recv_sem.at[1], above)

    for k in chunks:
        place(0, k, choose(k, 2))
    for k in chunks:
        own = choose(k, 0)
        arrived(zgot.at[k], recv_z.at[1, k])
        place(1, k, jnp.where(from_here, own, zgot[k]))

    arrived(wbuf.at[1, pl.ds(1, 3)], recv_sem.at[3])
    wbuf[2, 0] = wbuf[1, 0] + wbuf[1, 1] + wbuf[1, 2] + wbuf[1, 3]
    copy(wbuf.at[2, 0], wbuf.at[2, 1], send_sem.at[7], recv_sem.at[4], across)

    arrived(halo, recv_sem.at[0])
    arrived(field.at[0], recv_sem.at[1])

    has_below = jnp.full((32, 128), (tile > 0).astype(jnp.int32))
    has_above = jnp.full((32, 128), (tile < 15).astype(jnp.int32))

    def inside(i, value):
        if i < HALO:
            return jnp.where(has_below > 0, value, 0.0)
        if i >= HALO + 8:
            return jnp.where(has_above > 0, value, 0.0)
        return value

    for f in range(2):
        for i in (*range(HALO), *range(HALO + 8, 2 * HALO + 8)):
            field[f, i] = inside(i, field[f, i])

    def border(ref, start, width, i):
        if i < HALO:
            return halo[0, start + width - HALO + i]
        if i >= HALO + 8:
            return halo[1, start + i - HALO - 8]
        return ref[i - HALO]

    def sweep(i, v_at):
        here, low, up = v_at(i), v_at(i - 1), v_at(i + 1)
        k = kcon[i]
        kv = k * here
        near = low + up + shifted(here, 0, 0.0) + shifted(here, 1, 0.0)
        weighted = kcon[i - 1] * low + kcon[i + 1] * up + shifted(kv, 0, 0.0) + shifted(kv, 1, 0.0)
        return k, near, weighted, here

    for m in range(2):
        edge = 2 * m
        last = 2 * HALO + 8 - edge
        for i in range(edge, last):
            fresh = border(noise.at[m], 0 if m == 0 else 4, 4 if m == 0 else 2, i)
            value = inside(i, 0.8 * field[0, i] + 0.6 * fresh)
            prop[i] = value
            kcon[i] = jnp.exp(value)
        flag = jnp.full((32, 128), accept[m]) > 0
        for i in range(edge + 1, last - 1):
            k, near, weighted, here = sweep(i, lambda j: field[1, j])
            inv[i] = 0.8 / (6.0 * k + kcon[i - 1] + kcon[i + 1] + shifted(k, 0, 1.0) + shifted(k, 1, 1.0))
            value = 0.2 * here + (2.0 * border(source, 6, 3, i) + k * near + weighted) * inv[i]
            once[i] = inside(i, value)
        if m == 0:
            arrived(field.at[0], send_sem.at[4])
        for i in range(edge + 2, last - 2):
            k, near, weighted, here = sweep(i, lambda j: once[j])
            value = 0.2 * here + (2.0 * border(source, 6, 3, i) + k * near + weighted) * inv[i]
            field[0, i] = jnp.where(flag, prop[i], field[0, i])
            field[1, i] = jnp.where(flag, inside(i, value), field[1, i])

    final = field[1, interior]
    cond_out[...] = field[0, interior]
    pot_out[...] = final

    for d in range(1, 4):
        at = pl.ds(HALO + 2 * ((y + d) % 4), 2)
        copy(field.at[1, at], cols.at[0, d], send_sem.at[8], recv_rows.at[0, d], along(1, d))
    cols[0, 0] = field[1, pl.ds(HALO + 2 * y, 2)]
    scaled = final * weights[0]
    into = lax.broadcasted_iota(jnp.int32, (512, 512), 0)
    out = lax.broadcasted_iota(jnp.int32, (512, 512), 1)
    wanted = ((out // 16) % 4) * 128 + ((out // 64) % 2) * 64 + (out // 128) * 16 + out % 16
    select = jnp.where(into == wanted, 1.0, 0.0).astype(BF16)
    stacked = jnp.concatenate(
        [jnp.concatenate([scaled[4 * half + j] for j in range(4)], axis=1) for half in range(2)], axis=0
    )
    high, low = split(stacked)
    shuffled = jnp.dot(high, select, preferred_element_type=F32) + jnp.dot(low, select, preferred_element_type=F32)
    for j in range(4):
        for half in range(2):
            perm[j, half] = shuffled[32 * half : 32 * half + 32, 128 * j : 128 * j + 128]
    for d in range(1, 4):
        copy(perm.at[(x + d) % 4], rows.at[0, d], send_sem.at[9], recv_rows.at[1, d], along(0, d))
    rows[0, 0] = perm[x]

    def forward(src, axis, n):
        for d in range(1, 4):
            copy(src.at[0, n], src.at[d, n], send_sem.at[10 + axis], recv_rows.at[axis, 0], along(axis, d))

    forward(cols, 0, 0)
    forward(rows, 1, 0)
    for n in range(1, 4):
        arrived(cols.at[0, n], recv_rows.at[0, n])
        forward(cols, 0, n)
        arrived(rows.at[0, n], recv_rows.at[1, n])
        forward(rows, 1, n)
    arrived(cols.at[pl.ds(1, 3)], recv_rows.at[0, 0])
    arrived(rows.at[pl.ds(1, 3)], recv_rows.at[1, 0])

    right = jnp.concatenate(
        [jnp.concatenate([cols[dx, dy, 0], cols[dx, dy, 1]], axis=1) for dy in range(4) for dx in range(4)], axis=0
    )
    right_high, right_low = split(right)
    for half in range(2):
        left = jnp.concatenate([rows[dy, dx, half] for dy in range(4) for dx in range(4)], axis=0).T
        left_high, left_low = split(left)
        product = (
            jnp.dot(left_high, right_high, preferred_element_type=F32)
            + jnp.dot(left_high, right_low, preferred_element_type=F32)
            + jnp.dot(left_low, right_high, preferred_element_type=F32)
        )
        for c in range(2):
            partial[c, half] = product[64 * c : 64 * c + 64]
    copy(partial.at[1 - core], corner, send_sem.at[12], recv_sem.at[5], partner)
    arrived(corner, recv_sem.at[5])
    for half in range(2):
        total = partial[core, half] + corner[half]
        for j in range(4):
            summed[4 * half + j] = total[16 * j : 16 * j + 16]
    for d in sorted(range(1, 16), key=lambda d: -min(d, 16 - d)):
        copy(summed.at[(z + d) % 8], zsum.at[d], send_sem.at[13], recv_sem.at[6], device(x, y, (z + d) % 16, core))
    arrived(wbuf.at[2, 1], recv_sem.at[4])
    arrived(zsum.at[pl.ds(1, 15)], recv_sem.at[6])
    total = summed[z % 8]
    for d in range(1, 16):
        total = total + zsum[d]
    weight_sum = wbuf[2, 0] + wbuf[2, 1]
    piece = mom_out.at[pl.ds(pl.multiple_of(x * 16, 16), 16), pl.ds(pl.multiple_of(y * 256, 256), 256)]
    piece[...] = total / weight_sum[0:1, 0:1]
    for a in range(4):
        for b in range(4):
            if a or b:
                copy(piece, piece, send_sem.at[14], recv_sem.at[7], device((x + a) % 4, (y + b) % 4, z, core))
    arrived(zsum.at[pl.ds(1, 15)], recv_sem.at[7])
    many = zsum.at[pl.ds(1, 15)]
    three = rows.at[0, pl.ds(1, 3)]
    most = rows.at[pl.ds(1, 3)]
    works = wbuf.at[0, pl.ds(1, 3)]
    likes = (sent, sent, field.at[0], halo, None, works, works, wbuf.at[2, 1], three, three, most, most, corner, many, many)
    for i, like in enumerate(likes):
        if like is not None:
            arrived(like, send_sem.at[i])


def local(log_cond, potential, noise, source, parents, accept, weights):
    hbm = pl.BlockSpec(memory_space=pl.ANY)
    vmem, smem = pl.BlockSpec(memory_space=pltpu.VMEM), pl.BlockSpec(memory_space=pltpu.SMEM)
    dma = pltpu.SemaphoreType.DMA
    block = (8, 32, 128)
    part = (8 // CHUNKS, 32, 128)
    wide = (2 * HALO + 8, 32, 128)
    conduct, pot, moments = pl.pallas_call(
        kernel,
        out_shape=(
            pltpu.VMEM(block, F32),
            pltpu.VMEM(block, F32),
            pltpu.VMEM((64, 1024), F32),
        ),
        in_specs=[hbm, hbm, hbm, hbm, smem, smem, smem],
        out_specs=(vmem, vmem, vmem),
        scratch_shapes=[
            (pltpu.VMEM((4, *part), F32),) * CHUNKS,
            (pltpu.VMEM((8, *part), F32),) * CHUNKS,
            pltpu.VMEM((3, CHUNKS, 3, *part), F32),
            ((pltpu.VMEM((4, *part), F32),) * CHUNKS,) * 3,
            pltpu.VMEM((CHUNKS, *part), F32),
            pltpu.VMEM((CHUNKS, *part), F32),
            pltpu.VMEM((2, 9, 32, 128), F32),
            pltpu.VMEM((2, *wide), F32),
            pltpu.VMEM(wide, F32),
            pltpu.VMEM(wide, F32),
            pltpu.VMEM(wide, F32),
            pltpu.VMEM(wide, F32),
            pltpu.VMEM((2, *block), F32),
            pltpu.VMEM(block, F32),
            pltpu.VMEM((4, 2, 32, 128), F32),
            pltpu.VMEM((4, 4, 2, 32, 128), F32),
            pltpu.VMEM((4, 4, 2, 32, 128), F32),
            pltpu.VMEM((2, 2, 64, 256), F32),
            pltpu.VMEM((2, 64, 256), F32),
            pltpu.VMEM((8, 16, 256), F32),
            pltpu.VMEM((16, 16, 256), F32),
            pltpu.VMEM((3, 4, 8, 128), F32),
            dma((15,)), dma((3, CHUNKS)), dma((3, CHUNKS)), dma((2, CHUNKS)), dma((2, 4)), dma((8,)), dma((3,)),
        ],
        compiler_params=pltpu.CompilerParams(collective_id=0, has_side_effects=True),
        name="resample_move",
    )(log_cond[0], potential[0], noise[:, 0], source, parents, accept.reshape(-1), weights)
    return conduct[None], pot[None], moments


def solution(mesh):
    placed = (
        P("grp", "tile", None, None),
        P("grp", "tile", None, None),
        P(None, "grp", "tile", None, None),
        P("tile", None, None),
        P(),
        P(None, "grp"),
        P("grp"),
    )
    return jax.shard_map(
        local,
        mesh=mesh,
        in_specs=placed,
        out_specs=(P("grp", "tile", None, None), P("grp", "tile", None, None), P("tile", None)),
        check_vma=False,
    )
```

```python
import jax
import jax.numpy as jnp
from jax import lax
from jax.experimental import pallas as pl
from jax.experimental.pallas import tpu as pltpu
from jax.sharding import PartitionSpec as P

MESH = pl.DeviceIdType.MESH
F32 = jnp.float32
BF16 = jnp.bfloat16
CHUNKS = 4
HALO = 4


def device(x, y, z, core):
    return {"grp": (x * 4 + y) * 2 + z // 8, "tile": (z % 8) * 2 + core}


def split(value):
    high = value.astype(BF16)
    return high, (value - high.astype(F32)).astype(BF16)


def shifted(value, axis, fill):
    size = value.shape[axis]
    place = lax.broadcasted_iota(jnp.int32, value.shape, axis)
    up = jnp.where(place == 0, fill, pltpu.roll(value, 1, axis))
    down = jnp.where(place == size - 1, fill, pltpu.roll(value, size - 1, axis))
    return up + down


def kernel(
    log_cond, potential, noise_in, source_in, parents_in, accept_in, weights_in,
    cond_out, pot_out, mom_out,
    pot_got, cond_got, sent, picked, zsent, zgot, halo, field, prop, kcon, inv, once,
    parents, accept, weights, noise, source, perm, rows, cols, partial, corner, summed, zsum, wbuf,
    send_sem, recv_gather, recv_pick, recv_z, recv_rows, recv_sem, local_sem,
):
    group, tile = lax.axis_index("grp"), lax.axis_index("tile")
    x, y, z = group // 8, (group // 2) % 4, (group % 2) * 8 + tile // 2
    high_z, core = group % 2, tile % 2
    def copy(src, dst, sends, recvs, target):
        pltpu.make_async_remote_copy(
            src_ref=src, dst_ref=dst, send_sem=sends, recv_sem=recvs, device_id=target, device_id_type=MESH
        ).start()

    def arrived(like, sem):
        pltpu.make_async_copy(like, like, sem).wait()

    def along(axis, d):
        if axis == 0:
            return device((x + d) % 4, y, z, core)
        return device(x, (y + d) % 4, z, core)

    below = {"grp": (x * 4 + y) * 2 + ((z * 2 + core + 31) % 32) // 16, "tile": (tile + 15) % 16}
    above = {"grp": (x * 4 + y) * 2 + ((z * 2 + core + 1) % 32) // 16, "tile": (tile + 1) % 16}

    planes = 8 // CHUNKS
    chunk = [pl.ds(k * planes, planes) for k in range(CHUNKS)]
    chunks = range(CHUNKS)
    loads = [pltpu.make_async_copy(noise_in, noise, local_sem.at[0]), pltpu.make_async_copy(source_in, source, local_sem.at[0])]
    scalars = [
        pltpu.make_async_copy(src, dst, local_sem.at[3 + i])
        for i, (src, dst) in enumerate(((parents_in, parents), (accept_in, accept), (weights_in, weights)))
    ]
    for k in chunks:
        loads.append(pltpu.make_async_copy(potential.at[chunk[k]], pot_got[k].at[0], local_sem.at[1]))
        loads.append(pltpu.make_async_copy(log_cond.at[chunk[k]], cond_got[k].at[0], local_sem.at[2]))

    barrier = pltpu.get_barrier_semaphore()
    greeted = [device((x + a) % 4, (y + b) % 4, z, core) for a in range(4) for b in range(4) if a or b]
    greeted += [device(x, y, (z + d) % 16, core) for d in (8, 6, 10, 4, 12, 2, 14, 1, 15)]
    greeted += [device(x, y, (z + d) % 16, 1 - core) for d in (0, 1, 15)]
    for other in greeted:
        pl.semaphore_signal(barrier, inc=1, device_id=other, device_id_type=MESH)
    for c in scalars + loads:
        c.start()
    pl.semaphore_wait(barrier, len(greeted))

    across = device(x, y, (z + 8) % 16, core)
    for k in chunks:
        copy(log_cond.at[chunk[k]], cond_got[k].at[4], send_sem.at[2], recv_z.at[0, k], across)

    def gather(src, got, first, k, kind):
        for d in range(1, 4):
            copy(src, got.at[first + d], send_sem.at[0], recv_gather.at[kind, k], along(0, d))

    for k in chunks:
        gather(potential.at[chunk[k]], pot_got[k], 0, k, 0)

    for ref, start, width in ((noise_in.at[0], 0, 4), (noise_in.at[1], 4, 2), (source_in, 6, 3)):
        copy(ref.at[pl.ds(0, width)], halo.at[1, pl.ds(start, width)], send_sem.at[3], recv_sem.at[0], below)
        copy(ref.at[pl.ds(8 - width, width)], halo.at[0, pl.ds(start, width)], send_sem.at[3], recv_sem.at[0], above)
    for k in chunks:
        gather(log_cond.at[chunk[k]], cond_got[k], 0, k, 1)

    for c in scalars:
        c.wait()
    wbuf[0, 0] = jnp.full((8, 128), weights[0], F32)
    for d in range(1, 4):
        copy(wbuf.at[0, 0], wbuf.at[0, d], send_sem.at[5], recv_sem.at[2], along(0, d))

    def parent(a, b, c):
        return parents[(a * 4 + b) * 2 + c]

    def spread(k, kind):
        to_z = 1 - high_z if kind == 1 else high_z
        for d in (2, 1, 3, 0):
            p = parent(x, (y + d) % 4, to_z)
            slot = (x - p // 8 + 4) % 4
            if kind == 2:
                block = cond_got[k][((p + high_z) % 2) * 4 + slot]
            else:
                block = pot_got[k][slot]
            if d == 0:
                picked[kind][k][0] = block
            else:
                sent[kind, k, d - 1] = block
                copy(sent.at[kind, k, d - 1], picked[kind][k].at[d], send_sem.at[1], recv_pick.at[kind, k], along(1, d))

    def choose(k, kind):
        arrived(picked[kind][k].at[pl.ds(1, 3)], recv_pick.at[kind, k])
        p = parent(x, y, 1 - high_z if kind == 1 else high_z)
        return picked[kind][k][(y - (p // 2) % 4 + 4) % 4]

    arrived(sent.at[0], local_sem.at[0])
    arrived(noise.at[0], local_sem.at[1])
    arrived(noise.at[0], local_sem.at[2])
    for k in chunks:
        arrived(pot_got[k].at[pl.ds(1, 3)], recv_gather.at[0, k])
        spread(k, 1)
    for k in chunks:
        zsent[k] = choose(k, 1)
        copy(zsent.at[k], zgot.at[k], send_sem.at[2], recv_z.at[1, k], across)
    for k in chunks:
        spread(k, 0)
    for k in chunks:
        arrived(cond_got[k].at[4], recv_z.at[0, k])
        gather(cond_got[k].at[4], cond_got[k], 4, k, 2)

    arrived(wbuf.at[0, pl.ds(1, 3)], recv_sem.at[2])
    wbuf[1, 0] = wbuf[0, 0] + wbuf[0, 1] + wbuf[0, 2] + wbuf[0, 3]
    for d in range(1, 4):
        copy(wbuf.at[1, 0], wbuf.at[1, d], send_sem.at[6], recv_sem.at[3], along(1, d))

    for k in chunks:
        arrived(cond_got[k].at[pl.ds(1, 3)], recv_gather.at[1, k])
        arrived(cond_got[k].at[pl.ds(5, 3)], recv_gather.at[2, k])
        spread(k, 2)

    from_here = jnp.full((1, 32, 128), (parent(x, y, high_z) % 2 == high_z).astype(jnp.int32)) > 0
    interior = pl.ds(HALO, 8)

    def place(f, k, value):
        start = k * planes
        field[f, pl.ds(HALO + start, planes)] = value
        src = field.at[f, pl.ds(HALO + start, planes)]
        if start < HALO:
            copy(src, field.at[f, pl.ds(HALO + 8 + start, planes)], send_sem.at[4], recv_sem.at[1], below)
        else:
            copy(src, field.at[f, pl.ds(start - HALO, planes)], send_sem.at[4], recv_sem.at[1], above)

    for k in chunks:
        place(0, k, choose(k, 2))
    for k in chunks:
        own = choose(k, 0)
        arrived(zgot.at[k], recv_z.at[1, k])
        place(1, k, jnp.where(from_here, own, zgot[k]))

    arrived(wbuf.at[1, pl.ds(1, 3)], recv_sem.at[3])
    wbuf[2, 0] = wbuf[1, 0] + wbuf[1, 1] + wbuf[1, 2] + wbuf[1, 3]
    copy(wbuf.at[2, 0], wbuf.at[2, 1], send_sem.at[7], recv_sem.at[4], across)

    arrived(halo, recv_sem.at[0])
    arrived(field.at[0], recv_sem.at[1])

    has_below = jnp.full((32, 128), (tile > 0).astype(jnp.int32))
    has_above = jnp.full((32, 128), (tile < 15).astype(jnp.int32))

    def inside(i, value):
        if i < HALO:
            return jnp.where(has_below > 0, value, 0.0)
        if i >= HALO + 8:
            return jnp.where(has_above > 0, value, 0.0)
        return value

    for f in range(2):
        for i in (*range(HALO), *range(HALO + 8, 2 * HALO + 8)):
            field[f, i] = inside(i, field[f, i])

    def border(ref, start, width, i):
        if i < HALO:
            return halo[0, start + width - HALO + i]
        if i >= HALO + 8:
            return halo[1, start + i - HALO - 8]
        return ref[i - HALO]

    def sweep(i, v_at):
        here, low, up = v_at(i), v_at(i - 1), v_at(i + 1)
        k = kcon[i]
        kv = k * here
        near = low + up + shifted(here, 0, 0.0) + shifted(here, 1, 0.0)
        weighted = kcon[i - 1] * low + kcon[i + 1] * up + shifted(kv, 0, 0.0) + shifted(kv, 1, 0.0)
        return k, near, weighted, here

    for m in range(2):
        edge = 2 * m
        last = 2 * HALO + 8 - edge
        for i in range(edge, last):
            fresh = border(noise.at[m], 0 if m == 0 else 4, 4 if m == 0 else 2, i)
            value = inside(i, 0.8 * field[0, i] + 0.6 * fresh)
            prop[i] = value
            kcon[i] = jnp.exp(value)
        flag = jnp.full((32, 128), accept[m]) > 0
        for i in range(edge + 1, last - 1):
            k, near, weighted, here = sweep(i, lambda j: field[1, j])
            inv[i] = 0.8 / (6.0 * k + kcon[i - 1] + kcon[i + 1] + shifted(k, 0, 1.0) + shifted(k, 1, 1.0))
            value = 0.2 * here + (2.0 * border(source, 6, 3, i) + k * near + weighted) * inv[i]
            once[i] = inside(i, value)
        if m == 0:
            arrived(field.at[0], send_sem.at[4])
        for i in range(edge + 2, last - 2):
            k, near, weighted, here = sweep(i, lambda j: once[j])
            value = 0.2 * here + (2.0 * border(source, 6, 3, i) + k * near + weighted) * inv[i]
            field[0, i] = jnp.where(flag, prop[i], field[0, i])
            field[1, i] = jnp.where(flag, inside(i, value), field[1, i])

    final = field[1, interior]
    cond_out[...] = field[0, interior]
    pot_out[...] = final

    for d in range(1, 4):
        at = pl.ds(HALO + 2 * ((y + d) % 4), 2)
        copy(field.at[1, at], cols.at[0, d], send_sem.at[8], recv_rows.at[0, d], along(1, d))
    cols[0, 0] = field[1, pl.ds(HALO + 2 * y, 2)]
    scaled = final * weights[0]
    into = lax.broadcasted_iota(jnp.int32, (512, 512), 0)
    out = lax.broadcasted_iota(jnp.int32, (512, 512), 1)
    wanted = ((out // 16) % 4) * 128 + ((out // 64) % 2) * 64 + (out // 128) * 16 + out % 16
    select = jnp.where(into == wanted, 1.0, 0.0).astype(BF16)
    stacked = jnp.concatenate(
        [jnp.concatenate([scaled[4 * half + j] for j in range(4)], axis=1) for half in range(2)], axis=0
    )
    high, low = split(stacked)
    shuffled = jnp.dot(high, select, preferred_element_type=F32) + jnp.dot(low, select, preferred_element_type=F32)
    for j in range(4):
        for half in range(2):
            perm[j, half] = shuffled[32 * half : 32 * half + 32, 128 * j : 128 * j + 128]
    for d in range(1, 4):
        copy(perm.at[(x + d) % 4], rows.at[0, d], send_sem.at[9], recv_rows.at[1, d], along(0, d))
    rows[0, 0] = perm[x]

    def forward(src, axis, n):
        for d in range(1, 4):
            copy(src.at[0, n], src.at[d, n], send_sem.at[10 + axis], recv_rows.at[axis, 0], along(axis, d))

    forward(cols, 0, 0)
    forward(rows, 1, 0)
    for n in range(1, 4):
        arrived(cols.at[0, n], recv_rows.at[0, n])
        forward(cols, 0, n)
        arrived(rows.at[0, n], recv_rows.at[1, n])
        forward(rows, 1, n)
    arrived(cols.at[pl.ds(1, 3)], recv_rows.at[0, 0])
    arrived(rows.at[pl.ds(1, 3)], recv_rows.at[1, 0])

    right = jnp.concatenate(
        [jnp.concatenate([cols[dx, dy, 0], cols[dx, dy, 1]], axis=1) for dy in range(4) for dx in range(4)], axis=0
    )
    right_high, right_low = split(right)
    for half in range(2):
        left = jnp.concatenate([rows[dy, dx, half] for dy in range(4) for dx in range(4)], axis=0).T
        left_high, left_low = split(left)
        product = (
            jnp.dot(left_high, right_high, preferred_element_type=F32)
            + jnp.dot(left_high, right_low, preferred_element_type=F32)
            + jnp.dot(left_low, right_high, preferred_element_type=F32)
        )
        for c in range(2):
            for j in range(4):
                partial[j % 2, c, 2 * half + j // 2] = product[64 * c + 16 * j : 64 * c + 16 * j + 16]
    parity = z % 2
    beside = z + 1 - 2 * parity
    copy(partial.at[1 - parity, core], corner.at[1], send_sem.at[12], recv_sem.at[5], device(x, y, beside, core))
    copy(partial.at[1 - parity, 1 - core], corner.at[2], send_sem.at[12], recv_sem.at[5], device(x, y, beside, 1 - core))
    copy(partial.at[parity, 1 - core], corner.at[0], send_sem.at[12], recv_sem.at[5], device(x, y, z, 1 - core))
    arrived(corner, recv_sem.at[5])
    summed[...] = (partial[parity, core] + corner[0]) + (corner[1] + corner[2])
    for d in (8, 6, 10, 4, 12, 2, 14):
        copy(summed.at[((z + d) % 8) // 2], zsum.at[d // 2], send_sem.at[13], recv_sem.at[6], device(x, y, (z + d) % 16, core))
    arrived(wbuf.at[2, 1], recv_sem.at[4])
    arrived(zsum.at[pl.ds(1, 7)], recv_sem.at[6])
    total = summed[(z % 8) // 2]
    for d in range(1, 8):
        total = total + zsum[d]
    weight_sum = wbuf[2, 0] + wbuf[2, 1]
    piece = mom_out.at[pl.ds(pl.multiple_of(x * 16, 16), 16), pl.ds(pl.multiple_of(y * 256, 256), 256)]
    piece[...] = total / weight_sum[0:1, 0:1]
    for a in range(4):
        for b in range(4):
            if a or b:
                copy(piece, piece, send_sem.at[14], recv_sem.at[7], device((x + a) % 4, (y + b) % 4, z, core))
    arrived(zsum.at[pl.ds(1, 15)], recv_sem.at[7])
    many = zsum.at[pl.ds(1, 15)]
    three = rows.at[0, pl.ds(1, 3)]
    most = rows.at[pl.ds(1, 3)]
    works = wbuf.at[0, pl.ds(1, 3)]
    likes = (sent, sent, field.at[0], halo, None, works, works, wbuf.at[2, 1], three, three, most, most, corner, zsum.at[pl.ds(1, 7)], many)
    for i, like in enumerate(likes):
        if like is not None:
            arrived(like, send_sem.at[i])


def leave(cond, pot, mom, cond_out, pot_out, mom_out, sems):
    copies = [
        pltpu.make_async_copy(src, dst, sems.at[i])
        for i, (src, dst) in enumerate(((mom, mom_out), (cond, cond_out), (pot, pot_out)))
    ]
    for c in copies:
        c.start()
    for c in copies:
        c.wait()


def local(log_cond, potential, noise, source, parents, accept, weights):
    hbm = pl.BlockSpec(memory_space=pl.ANY)
    vmem = pl.BlockSpec(memory_space=pltpu.VMEM)
    dma = pltpu.SemaphoreType.DMA
    block = (8, 32, 128)
    part = (8 // CHUNKS, 32, 128)
    wide = (2 * HALO + 8, 32, 128)
    conduct, pot, moments = pl.pallas_call(
        kernel,
        out_shape=(
            pltpu.VMEM(block, F32),
            pltpu.VMEM(block, F32),
            pltpu.VMEM((64, 1024), F32),
        ),
        in_specs=[hbm] * 7,
        out_specs=(vmem, vmem, vmem),
        scratch_shapes=[
            (pltpu.VMEM((4, *part), F32),) * CHUNKS,
            (pltpu.VMEM((8, *part), F32),) * CHUNKS,
            pltpu.VMEM((3, CHUNKS, 3, *part), F32),
            ((pltpu.VMEM((4, *part), F32),) * CHUNKS,) * 3,
            pltpu.VMEM((CHUNKS, *part), F32),
            pltpu.VMEM((CHUNKS, *part), F32),
            pltpu.VMEM((2, 9, 32, 128), F32),
            pltpu.VMEM((2, *wide), F32),
            pltpu.VMEM(wide, F32),
            pltpu.VMEM(wide, F32),
            pltpu.VMEM(wide, F32),
            pltpu.VMEM(wide, F32),
            pltpu.SMEM((32,), jnp.int32),
            pltpu.SMEM((2,), jnp.int32),
            pltpu.SMEM((1,), F32),
            pltpu.VMEM((2, *block), F32),
            pltpu.VMEM(block, F32),
            pltpu.VMEM((4, 2, 32, 128), F32),
            pltpu.VMEM((4, 4, 2, 32, 128), F32),
            pltpu.VMEM((4, 4, 2, 32, 128), F32),
            pltpu.VMEM((2, 2, 4, 16, 256), F32),
            pltpu.VMEM((3, 4, 16, 256), F32),
            pltpu.VMEM((4, 16, 256), F32),
            pltpu.VMEM((16, 16, 256), F32),
            pltpu.VMEM((3, 4, 8, 128), F32),
            dma((15,)), dma((3, CHUNKS)), dma((3, CHUNKS)), dma((2, CHUNKS)), dma((2, 4)), dma((8,)), dma((6,)),
        ],
        compiler_params=pltpu.CompilerParams(collective_id=0, has_side_effects=True),
        name="resample_move",
    )(log_cond[0], potential[0], noise[:, 0], source, parents, accept.reshape(-1), weights)
    conduct, pot, moments = pl.pallas_call(
        leave,
        out_shape=(
            jax.ShapeDtypeStruct(block, F32),
            jax.ShapeDtypeStruct(block, F32),
            jax.ShapeDtypeStruct((64, 1024), F32),
        ),
        in_specs=[hbm] * 3,
        out_specs=(hbm, hbm, hbm),
        scratch_shapes=[dma((3,))],
        name="leave",
    )(*(pltpu.with_memory_space_constraint(value, pltpu.VMEM) for value in (conduct, pot, moments)))
    return conduct[None], pot[None], moments


def solution(mesh):
    placed = (
        P("grp", "tile", None, None),
        P("grp", "tile", None, None),
        P(None, "grp", "tile", None, None),
        P("tile", None, None),
        P(),
        P(None, "grp"),
        P("grp"),
    )
    return jax.shard_map(
        local,
        mesh=mesh,
        in_specs=placed,
        out_specs=(P("grp", "tile", None, None), P("grp", "tile", None, None), P("tile", None)),
        check_vma=False,
    )
```

```python
import jax
import jax.numpy as jnp
from jax import lax
from jax.experimental import pallas as pl
from jax.experimental.pallas import tpu as pltpu
from jax.sharding import PartitionSpec as P

MESH = pl.DeviceIdType.MESH
F32 = jnp.float32
BF16 = jnp.bfloat16
CHUNKS = 4
HALO = 4
FAR_FIRST = (2, 1, 3)


def device(x, y, z, core):
    return {"grp": (x * 4 + y) * 2 + z // 8, "tile": (z % 8) * 2 + core}


def split(value):
    high = value.astype(BF16)
    return high, (value - high.astype(F32)).astype(BF16)


def shifted(value, axis, fill):
    size = value.shape[axis]
    place = lax.broadcasted_iota(jnp.int32, value.shape, axis)
    up = jnp.where(place == 0, fill, pltpu.roll(value, 1, axis))
    down = jnp.where(place == size - 1, fill, pltpu.roll(value, size - 1, axis))
    return up + down


def kernel(
    log_cond, potential, noise_in, source_in, parents_in, accept_in, weights_in,
    cond_out, pot_out, mom_out,
    pot_got, cond_got, sent, picked, zsent, zgot, halo, field, prop, kcon, inv, once,
    parents, accept, weights, noise, source, select, perm, rows, cols, partial, corner, summed, zsum, wbuf,
    send_sem, recv_gather, recv_pick, recv_z, recv_rows, recv_pair, recv_sem, local_sem,
):
    group, tile = lax.axis_index("grp"), lax.axis_index("tile")
    x, y, z = group // 8, (group // 2) % 4, (group % 2) * 8 + tile // 2
    high_z, core = group % 2, tile % 2
    def copy(src, dst, sends, recvs, target):
        pltpu.make_async_remote_copy(
            src_ref=src, dst_ref=dst, send_sem=sends, recv_sem=recvs, device_id=target, device_id_type=MESH
        ).start()

    def arrived(like, sem):
        pltpu.make_async_copy(like, like, sem).wait()

    def along(axis, d):
        if axis == 0:
            return device((x + d) % 4, y, z, core)
        return device(x, (y + d) % 4, z, core)

    below = {"grp": (x * 4 + y) * 2 + ((z * 2 + core + 31) % 32) // 16, "tile": (tile + 15) % 16}
    above = {"grp": (x * 4 + y) * 2 + ((z * 2 + core + 1) % 32) // 16, "tile": (tile + 1) % 16}

    planes = 8 // CHUNKS
    chunk = [pl.ds(k * planes, planes) for k in range(CHUNKS)]
    chunks = range(CHUNKS)
    loads = [pltpu.make_async_copy(noise_in, noise, local_sem.at[0]), pltpu.make_async_copy(source_in, source, local_sem.at[0])]
    scalars = [
        pltpu.make_async_copy(src, dst, local_sem.at[3 + i])
        for i, (src, dst) in enumerate(((parents_in, parents), (accept_in, accept), (weights_in, weights)))
    ]
    for k in chunks:
        loads.append(pltpu.make_async_copy(potential.at[chunk[k]], pot_got[k].at[0], local_sem.at[1]))
        loads.append(pltpu.make_async_copy(log_cond.at[chunk[k]], cond_got[k].at[0], local_sem.at[2]))

    barrier = pltpu.get_barrier_semaphore()
    greeted = [device((x + a) % 4, (y + b) % 4, z, core) for a in range(4) for b in range(4) if a or b]
    greeted += [device(x, y, (z + d) % 16, core) for d in (8, 6, 10, 4, 12, 2, 14, 1, 15)]
    greeted += [device(x, y, (z + d) % 16, 1 - core) for d in (0, 1, 15)]
    for other in greeted:
        pl.semaphore_signal(barrier, inc=1, device_id=other, device_id_type=MESH)
    for c in scalars + loads:
        c.start()
    pl.semaphore_wait(barrier, len(greeted))

    across = device(x, y, (z + 8) % 16, core)
    for k in chunks:
        copy(log_cond.at[chunk[k]], cond_got[k].at[4], send_sem.at[2], recv_z.at[0, k], across)

    def gather(src, got, first, k, kind):
        for d in FAR_FIRST:
            copy(src, got.at[first + d], send_sem.at[0], recv_gather.at[kind, k], along(0, d))

    for k in chunks:
        gather(potential.at[chunk[k]], pot_got[k], 0, k, 0)

    for ref, start, width in ((noise_in.at[0], 0, 4), (noise_in.at[1], 4, 2), (source_in, 6, 3)):
        copy(ref.at[pl.ds(0, width)], halo.at[1, pl.ds(start, width)], send_sem.at[3], recv_sem.at[0], below)
        copy(ref.at[pl.ds(8 - width, width)], halo.at[0, pl.ds(start, width)], send_sem.at[3], recv_sem.at[0], above)
    for k in chunks:
        gather(log_cond.at[chunk[k]], cond_got[k], 0, k, 1)

    for c in scalars:
        c.wait()
    wbuf[0, 0] = jnp.full((8, 128), weights[0], F32)
    for d in range(1, 4):
        copy(wbuf.at[0, 0], wbuf.at[0, d], send_sem.at[5], recv_sem.at[2], along(0, d))

    def parent(a, b, c):
        return parents[(a * 4 + b) * 2 + c]

    def spread(k, kind):
        to_z = 1 - high_z if kind == 1 else high_z
        for d in (*FAR_FIRST, 0):
            p = parent(x, (y + d) % 4, to_z)
            slot = (x - p // 8 + 4) % 4
            if kind == 2:
                block = cond_got[k][((p + high_z) % 2) * 4 + slot]
            else:
                block = pot_got[k][slot]
            if d == 0:
                picked[kind][k][0] = block
            else:
                sent[kind, k, d - 1] = block
                copy(sent.at[kind, k, d - 1], picked[kind][k].at[d], send_sem.at[1], recv_pick.at[kind, k], along(1, d))

    def choose(k, kind):
        arrived(picked[kind][k].at[pl.ds(1, 3)], recv_pick.at[kind, k])
        p = parent(x, y, 1 - high_z if kind == 1 else high_z)
        return picked[kind][k][(y - (p // 2) % 4 + 4) % 4]

    arrived(sent.at[0], local_sem.at[0])
    arrived(noise.at[0], local_sem.at[1])
    arrived(noise.at[0], local_sem.at[2])
    def cross(k):
        arrived(pot_got[k].at[pl.ds(1, 3)], recv_gather.at[0, k])
        spread(k, 1)

    def leave_side(k):
        zsent[k] = choose(k, 1)
        copy(zsent.at[k], zgot.at[k], send_sem.at[2], recv_z.at[1, k], across)

    def pass_on(k):
        arrived(cond_got[k].at[4], recv_z.at[0, k])
        gather(cond_got[k].at[4], cond_got[k], 4, k, 2)

    cross(0)
    cross(1)
    leave_side(0)
    cross(2)
    leave_side(1)
    cross(3)
    pass_on(0)
    leave_side(2)
    pass_on(1)
    leave_side(3)
    for k in chunks:
        spread(k, 0)
    pass_on(2)
    pass_on(3)

    arrived(wbuf.at[0, pl.ds(1, 3)], recv_sem.at[2])
    wbuf[1, 0] = wbuf[0, 0] + wbuf[0, 1] + wbuf[0, 2] + wbuf[0, 3]
    for d in range(1, 4):
        copy(wbuf.at[1, 0], wbuf.at[1, d], send_sem.at[6], recv_sem.at[3], along(1, d))

    for k in chunks:
        arrived(cond_got[k].at[pl.ds(1, 3)], recv_gather.at[1, k])
        arrived(cond_got[k].at[pl.ds(5, 3)], recv_gather.at[2, k])
        spread(k, 2)

    from_here = jnp.full((1, 32, 128), (parent(x, y, high_z) % 2 == high_z).astype(jnp.int32)) > 0
    interior = pl.ds(HALO, 8)

    def place(f, k, value):
        start = k * planes
        field[f, pl.ds(HALO + start, planes)] = value
        src = field.at[f, pl.ds(HALO + start, planes)]
        if start < HALO:
            copy(src, field.at[f, pl.ds(HALO + 8 + start, planes)], send_sem.at[4], recv_sem.at[1], below)
        else:
            copy(src, field.at[f, pl.ds(start - HALO, planes)], send_sem.at[4], recv_sem.at[1], above)

    for k in chunks:
        place(0, k, choose(k, 2))
    for k in chunks:
        own = choose(k, 0)
        arrived(zgot.at[k], recv_z.at[1, k])
        place(1, k, jnp.where(from_here, own, zgot[k]))

    arrived(wbuf.at[1, pl.ds(1, 3)], recv_sem.at[3])
    wbuf[2, 0] = wbuf[1, 0] + wbuf[1, 1] + wbuf[1, 2] + wbuf[1, 3]
    copy(wbuf.at[2, 0], wbuf.at[2, 1], send_sem.at[7], recv_sem.at[4], across)

    into = lax.broadcasted_iota(jnp.int32, (512, 512), 0)
    out = lax.broadcasted_iota(jnp.int32, (512, 512), 1)
    wanted = ((out // 16) % 4) * 128 + ((out // 64) % 2) * 64 + (out // 128) * 16 + out % 16
    select[...] = jnp.where(into == wanted, 1.0, 0.0).astype(BF16)
    arrived(halo, recv_sem.at[0])
    arrived(field.at[0], recv_sem.at[1])

    has_below = jnp.full((32, 128), (tile > 0).astype(jnp.int32))
    has_above = jnp.full((32, 128), (tile < 15).astype(jnp.int32))

    def inside(i, value):
        if i < HALO:
            return jnp.where(has_below > 0, value, 0.0)
        if i >= HALO + 8:
            return jnp.where(has_above > 0, value, 0.0)
        return value

    for f in range(2):
        for i in (*range(HALO), *range(HALO + 8, 2 * HALO + 8)):
            field[f, i] = inside(i, field[f, i])

    def border(ref, start, width, i):
        if i < HALO:
            return halo[0, start + width - HALO + i]
        if i >= HALO + 8:
            return halo[1, start + i - HALO - 8]
        return ref[i - HALO]

    def sweep(i, v_at):
        here, low, up = v_at(i), v_at(i - 1), v_at(i + 1)
        k = kcon[i]
        kv = k * here
        near = low + up + shifted(here, 0, 0.0) + shifted(here, 1, 0.0)
        weighted = kcon[i - 1] * low + kcon[i + 1] * up + shifted(kv, 0, 0.0) + shifted(kv, 1, 0.0)
        return k, near, weighted, here

    for m in range(2):
        edge = 2 * m
        last = 2 * HALO + 8 - edge
        for i in range(edge, last):
            fresh = border(noise.at[m], 0 if m == 0 else 4, 4 if m == 0 else 2, i)
            value = inside(i, 0.8 * field[0, i] + 0.6 * fresh)
            prop[i] = value
            kcon[i] = jnp.exp(value)
        flag = jnp.full((32, 128), accept[m]) > 0
        for i in range(edge + 1, last - 1):
            k, near, weighted, here = sweep(i, lambda j: field[1, j])
            inv[i] = 0.8 / (6.0 * k + kcon[i - 1] + kcon[i + 1] + shifted(k, 0, 1.0) + shifted(k, 1, 1.0))
            value = 0.2 * here + (2.0 * border(source, 6, 3, i) + k * near + weighted) * inv[i]
            once[i] = inside(i, value)
        if m == 0:
            arrived(field.at[0], send_sem.at[4])
        for i in range(edge + 2, last - 2):
            k, near, weighted, here = sweep(i, lambda j: once[j])
            value = 0.2 * here + (2.0 * border(source, 6, 3, i) + k * near + weighted) * inv[i]
            field[0, i] = jnp.where(flag, prop[i], field[0, i])
            field[1, i] = jnp.where(flag, inside(i, value), field[1, i])

    final = field[1, interior]
    cond_out[...] = field[0, interior]
    pot_out[...] = final

    for d in FAR_FIRST:
        at = pl.ds(HALO + 2 * ((y + d) % 4), 2)
        copy(field.at[1, at], cols.at[0, d], send_sem.at[8], recv_rows.at[0, d], along(1, d))
    cols[0, 0] = field[1, pl.ds(HALO + 2 * y, 2)]
    scaled = final * weights[0]
    stacked = jnp.concatenate(
        [jnp.concatenate([scaled[4 * half + j] for j in range(4)], axis=1) for half in range(2)], axis=0
    )
    high, low = split(stacked)
    shuffled = jnp.dot(high, select[...], preferred_element_type=F32) + jnp.dot(low, select[...], preferred_element_type=F32)
    for j in range(4):
        for half in range(2):
            perm[j, half] = shuffled[32 * half : 32 * half + 32, 128 * j : 128 * j + 128]
    for d in FAR_FIRST:
        copy(perm.at[(x + d) % 4], rows.at[0, d], send_sem.at[9], recv_rows.at[1, d], along(0, d))
    rows[0, 0] = perm[x]

    def forward(src, axis, n):
        for d in FAR_FIRST:
            copy(src.at[0, n], src.at[d, n], send_sem.at[10 + axis], recv_rows.at[axis, 0], along(axis, d))

    forward(cols, 0, 0)
    forward(rows, 1, 0)
    for n in (1, 3, 2):
        arrived(cols.at[0, n], recv_rows.at[0, n])
        forward(cols, 0, n)
        arrived(rows.at[0, n], recv_rows.at[1, n])
        forward(rows, 1, n)
    arrived(cols.at[pl.ds(1, 3)], recv_rows.at[0, 0])
    arrived(rows.at[pl.ds(1, 3)], recv_rows.at[1, 0])

    right = jnp.concatenate(
        [jnp.concatenate([cols[dx, dy, 0], cols[dx, dy, 1]], axis=1) for dy in range(4) for dx in range(4)], axis=0
    )
    right_high, right_low = split(right)
    lefts = [split(jnp.concatenate([rows[dy, dx, half] for dy in range(4) for dx in range(4)], axis=0).T) for half in range(2)]

    parity = z % 2
    beside = z + 1 - 2 * parity
    for h in range(2):
        lanes = slice(128 * h, 128 * h + 128)
        for half in range(2):
            left_high, left_low = lefts[half]
            product = (
                jnp.dot(left_high, right_high[:, lanes], preferred_element_type=F32)
                + jnp.dot(left_high, right_low[:, lanes], preferred_element_type=F32)
                + jnp.dot(left_low, right_high[:, lanes], preferred_element_type=F32)
            )
            for c in range(2):
                for j in range(4):
                    partial[h, j % 2, c, 2 * half + j // 2] = product[64 * c + 16 * j : 64 * c + 16 * j + 16]
        for i, (across_z, other) in enumerate(((False, True), (True, False), (True, True))):
            src = partial.at[h, 1 - parity if across_z else parity, 1 - core if other else core]
            target = device(x, y, beside if across_z else z, 1 - core if other else core)
            copy(src, corner.at[h, i], send_sem.at[12], recv_pair.at[0, h], target)
    for h in range(2):
        arrived(corner.at[h], recv_pair.at[0, h])
        summed[h] = (partial[h, parity, core] + corner[h, 0]) + (corner[h, 1] + corner[h, 2])
        for d in (8, 6, 10, 4, 12, 2, 14):
            target = device(x, y, (z + d) % 16, core)
            copy(summed.at[h, ((z + d) % 8) // 2], zsum.at[h, d // 2], send_sem.at[13], recv_pair.at[1, h], target)
    arrived(wbuf.at[2, 1], recv_sem.at[4])
    weight_sum = (wbuf[2, 0] + wbuf[2, 1])[0:1, 0:1]
    for h in range(2):
        arrived(zsum.at[h, pl.ds(1, 7)], recv_pair.at[1, h])
        total = summed[h, (z % 8) // 2]
        for d in range(1, 8):
            total = total + zsum[h, d]
        piece = mom_out.at[pl.ds(pl.multiple_of(x * 16, 16), 16), pl.ds(pl.multiple_of(y * 256 + 128 * h, 128), 128)]
        piece[...] = total / weight_sum
        for a in (2, 1, 3, 0):
            for b in (2, 1, 3, 0):
                if a or b:
                    copy(piece, piece, send_sem.at[14], recv_sem.at[7], device((x + a) % 4, (y + b) % 4, z, core))
    many = zsum.at[pl.ds(0, 2), pl.ds(1, 15)]
    arrived(many, recv_sem.at[7])
    three = rows.at[0, pl.ds(1, 3)]
    most = rows.at[pl.ds(1, 3)]
    works = wbuf.at[0, pl.ds(1, 3)]
    likes = (sent, sent, field.at[0], halo, None, works, works, wbuf.at[2, 1], three, three, most, most, corner, zsum.at[pl.ds(0, 2), pl.ds(1, 7)], many)
    for i, like in enumerate(likes):
        if like is not None:
            arrived(like, send_sem.at[i])


def leave(cond, pot, mom, cond_out, pot_out, mom_out, sems):
    copies = [
        pltpu.make_async_copy(src, dst, sems.at[i])
        for i, (src, dst) in enumerate(((mom, mom_out), (cond, cond_out), (pot, pot_out)))
    ]
    for c in copies:
        c.start()
    for c in copies:
        c.wait()


def local(log_cond, potential, noise, source, parents, accept, weights):
    hbm = pl.BlockSpec(memory_space=pl.ANY)
    vmem = pl.BlockSpec(memory_space=pltpu.VMEM)
    dma = pltpu.SemaphoreType.DMA
    block = (8, 32, 128)
    part = (8 // CHUNKS, 32, 128)
    wide = (2 * HALO + 8, 32, 128)
    conduct, pot, moments = pl.pallas_call(
        kernel,
        out_shape=(
            pltpu.VMEM(block, F32),
            pltpu.VMEM(block, F32),
            pltpu.VMEM((64, 1024), F32),
        ),
        in_specs=[hbm] * 4 + [pl.BlockSpec(memory_space=pltpu.HBM)] * 3,
        out_specs=(vmem, vmem, vmem),
        scratch_shapes=[
            (pltpu.VMEM((4, *part), F32),) * CHUNKS,
            (pltpu.VMEM((8, *part), F32),) * CHUNKS,
            pltpu.VMEM((3, CHUNKS, 3, *part), F32),
            ((pltpu.VMEM((4, *part), F32),) * CHUNKS,) * 3,
            pltpu.VMEM((CHUNKS, *part), F32),
            pltpu.VMEM((CHUNKS, *part), F32),
            pltpu.VMEM((2, 9, 32, 128), F32),
            pltpu.VMEM((2, *wide), F32),
            pltpu.VMEM(wide, F32),
            pltpu.VMEM(wide, F32),
            pltpu.VMEM(wide, F32),
            pltpu.VMEM(wide, F32),
            pltpu.SMEM((32,), jnp.int32),
            pltpu.SMEM((2,), jnp.int32),
            pltpu.SMEM((1,), F32),
            pltpu.VMEM((2, *block), F32),
            pltpu.VMEM(block, F32),
            pltpu.VMEM((512, 512), BF16),
            pltpu.VMEM((4, 2, 32, 128), F32),
            pltpu.VMEM((4, 4, 2, 32, 128), F32),
            pltpu.VMEM((4, 4, 2, 32, 128), F32),
            pltpu.VMEM((2, 2, 2, 4, 16, 128), F32),
            pltpu.VMEM((2, 3, 4, 16, 128), F32),
            pltpu.VMEM((2, 4, 16, 128), F32),
            pltpu.VMEM((2, 16, 16, 128), F32),
            pltpu.VMEM((3, 4, 8, 128), F32),
            dma((15,)), dma((3, CHUNKS)), dma((3, CHUNKS)), dma((2, CHUNKS)), dma((2, 4)), dma((2, 2)), dma((8,)), dma((6,)),
        ],
        compiler_params=pltpu.CompilerParams(collective_id=0, has_side_effects=True),
        name="resample_move",
    )(log_cond[0], potential[0], noise[:, 0], source, parents, accept.reshape(-1), weights)
    conduct, pot, moments = pl.pallas_call(
        leave,
        out_shape=(
            jax.ShapeDtypeStruct(block, F32),
            jax.ShapeDtypeStruct(block, F32),
            jax.ShapeDtypeStruct((64, 1024), F32),
        ),
        in_specs=[hbm] * 3,
        out_specs=(hbm, hbm, hbm),
        scratch_shapes=[dma((3,))],
        name="leave",
    )(*(pltpu.with_memory_space_constraint(value, pltpu.VMEM) for value in (conduct, pot, moments)))
    return conduct[None], pot[None], moments


def solution(mesh):
    placed = (
        P("grp", "tile", None, None),
        P("grp", "tile", None, None),
        P(None, "grp", "tile", None, None),
        P("tile", None, None),
        P(),
        P(None, "grp"),
        P("grp"),
    )
    return jax.shard_map(
        local,
        mesh=mesh,
        in_specs=placed,
        out_specs=(P("grp", "tile", None, None), P("grp", "tile", None, None), P("tile", None)),
        check_vma=False,
    )
```

```python
import jax
import jax.numpy as jnp
from jax import lax
from jax.experimental import pallas as pl
from jax.experimental.pallas import tpu as pltpu
from jax.sharding import PartitionSpec as P

MESH = pl.DeviceIdType.MESH
F32 = jnp.float32
BF16 = jnp.bfloat16
CHUNKS = 4
HALO = 4
FAR_FIRST = (2, 1, 3)


def device(x, y, z, core):
    return {"grp": (x * 4 + y) * 2 + z // 8, "tile": (z % 8) * 2 + core}


def split(value):
    high = value.astype(BF16)
    return high, (value - high.astype(F32)).astype(BF16)


def shifted(value, axis, fill):
    size = value.shape[axis]
    place = lax.broadcasted_iota(jnp.int32, value.shape, axis)
    up = jnp.where(place == 0, fill, pltpu.roll(value, 1, axis))
    down = jnp.where(place == size - 1, fill, pltpu.roll(value, size - 1, axis))
    return up + down


def kernel(
    log_cond, potential, noise_in, source_in, parents_in, accept_in, weights_in,
    cond_out, pot_out, mom_out,
    pot_got, cond_got, sent, picked, zsent, zgot, halo, field, prop, kcon, inv, once,
    parents, accept, weights, noise, source, select, perm, rows, cols, partial, corner, both, summed, zsum, wbuf,
    send_sem, recv_gather, recv_pick, recv_z, recv_rows, recv_pair, recv_sem, local_sem,
):
    group, tile = lax.axis_index("grp"), lax.axis_index("tile")
    x, y, z = group // 8, (group // 2) % 4, (group % 2) * 8 + tile // 2
    high_z, core = group % 2, tile % 2
    def copy(src, dst, sends, recvs, target):
        pltpu.make_async_remote_copy(
            src_ref=src, dst_ref=dst, send_sem=sends, recv_sem=recvs, device_id=target, device_id_type=MESH
        ).start()

    def arrived(like, sem):
        pltpu.make_async_copy(like, like, sem).wait()

    def along(axis, d):
        if axis == 0:
            return device((x + d) % 4, y, z, core)
        return device(x, (y + d) % 4, z, core)

    below = {"grp": (x * 4 + y) * 2 + ((z * 2 + core + 31) % 32) // 16, "tile": (tile + 15) % 16}
    above = {"grp": (x * 4 + y) * 2 + ((z * 2 + core + 1) % 32) // 16, "tile": (tile + 1) % 16}

    planes = 8 // CHUNKS
    chunk = [pl.ds(k * planes, planes) for k in range(CHUNKS)]
    chunks = range(CHUNKS)
    loads = [pltpu.make_async_copy(noise_in, noise, local_sem.at[0]), pltpu.make_async_copy(source_in, source, local_sem.at[0])]
    scalars = [
        pltpu.make_async_copy(src, dst, local_sem.at[3 + i])
        for i, (src, dst) in enumerate(((parents_in, parents), (accept_in, accept), (weights_in, weights)))
    ]
    for k in chunks:
        loads.append(pltpu.make_async_copy(potential.at[chunk[k]], pot_got[k].at[0], local_sem.at[1]))
        loads.append(pltpu.make_async_copy(log_cond.at[chunk[k]], cond_got[k].at[0], local_sem.at[2]))

    barrier = pltpu.get_barrier_semaphore()
    greeted = [device((x + a) % 4, (y + b) % 4, z, core) for a in range(4) for b in range(4) if a or b]
    greeted += [device(x, y, (z + d) % 16, core) for d in (8, 6, 10, 4, 12, 2, 14, 1, 15)]
    greeted += [device(x, y, (z + d) % 16, 1 - core) for d in (0, 1, 15)]
    for other in greeted:
        pl.semaphore_signal(barrier, inc=1, device_id=other, device_id_type=MESH)
    for c in scalars + loads:
        c.start()
    pl.semaphore_wait(barrier, len(greeted))

    across = device(x, y, (z + 8) % 16, core)
    for k in chunks:
        copy(log_cond.at[chunk[k]], cond_got[k].at[4], send_sem.at[2], recv_z.at[0, k], across)

    def gather(src, got, first, k, kind):
        for d in FAR_FIRST:
            copy(src, got.at[first + d], send_sem.at[0], recv_gather.at[kind, k], along(0, d))

    for k in chunks:
        gather(potential.at[chunk[k]], pot_got[k], 0, k, 0)

    for ref, start, width in ((noise_in.at[0], 0, 4), (noise_in.at[1], 4, 2), (source_in, 6, 3)):
        copy(ref.at[pl.ds(0, width)], halo.at[1, pl.ds(start, width)], send_sem.at[3], recv_sem.at[0], below)
        copy(ref.at[pl.ds(8 - width, width)], halo.at[0, pl.ds(start, width)], send_sem.at[3], recv_sem.at[0], above)
    for k in chunks:
        gather(log_cond.at[chunk[k]], cond_got[k], 0, k, 1)

    for c in scalars:
        c.wait()
    wbuf[0, 0] = jnp.full((8, 128), weights[0], F32)
    for d in range(1, 4):
        copy(wbuf.at[0, 0], wbuf.at[0, d], send_sem.at[5], recv_sem.at[2], along(0, d))

    def parent(a, b, c):
        return parents[(a * 4 + b) * 2 + c]

    def spread(k, kind):
        to_z = 1 - high_z if kind == 1 else high_z
        for d in (*FAR_FIRST, 0):
            p = parent(x, (y + d) % 4, to_z)
            slot = (x - p // 8 + 4) % 4
            if kind == 2:
                block = cond_got[k][((p + high_z) % 2) * 4 + slot]
            else:
                block = pot_got[k][slot]
            if d == 0:
                picked[kind][k][0] = block
            else:
                sent[kind, k, d - 1] = block
                copy(sent.at[kind, k, d - 1], picked[kind][k].at[d], send_sem.at[1], recv_pick.at[kind, k], along(1, d))

    def choose(k, kind):
        arrived(picked[kind][k].at[pl.ds(1, 3)], recv_pick.at[kind, k])
        p = parent(x, y, 1 - high_z if kind == 1 else high_z)
        return picked[kind][k][(y - (p // 2) % 4 + 4) % 4]

    arrived(sent.at[0], local_sem.at[0])
    arrived(noise.at[0], local_sem.at[1])
    arrived(noise.at[0], local_sem.at[2])
    def cross(k):
        arrived(pot_got[k].at[pl.ds(1, 3)], recv_gather.at[0, k])
        spread(k, 1)

    def leave_side(k):
        zsent[k] = choose(k, 1)
        copy(zsent.at[k], zgot.at[k], send_sem.at[2], recv_z.at[1, k], across)

    def pass_on(k):
        arrived(cond_got[k].at[4], recv_z.at[0, k])
        gather(cond_got[k].at[4], cond_got[k], 4, k, 2)

    cross(0)
    cross(1)
    leave_side(0)
    cross(2)
    leave_side(1)
    cross(3)
    pass_on(0)
    leave_side(2)
    pass_on(1)
    leave_side(3)
    for k in chunks:
        spread(k, 0)
    pass_on(2)
    pass_on(3)

    arrived(wbuf.at[0, pl.ds(1, 3)], recv_sem.at[2])
    wbuf[1, 0] = wbuf[0, 0] + wbuf[0, 1] + wbuf[0, 2] + wbuf[0, 3]
    for d in range(1, 4):
        copy(wbuf.at[1, 0], wbuf.at[1, d], send_sem.at[6], recv_sem.at[3], along(1, d))

    for k in chunks:
        arrived(cond_got[k].at[pl.ds(1, 3)], recv_gather.at[1, k])
        arrived(cond_got[k].at[pl.ds(5, 3)], recv_gather.at[2, k])
        spread(k, 2)

    from_here = jnp.full((1, 32, 128), (parent(x, y, high_z) % 2 == high_z).astype(jnp.int32)) > 0
    interior = pl.ds(HALO, 8)

    def place(f, k, value):
        start = k * planes
        field[f, pl.ds(HALO + start, planes)] = value
        src = field.at[f, pl.ds(HALO + start, planes)]
        if start < HALO:
            copy(src, field.at[f, pl.ds(HALO + 8 + start, planes)], send_sem.at[4], recv_sem.at[1], below)
        else:
            copy(src, field.at[f, pl.ds(start - HALO, planes)], send_sem.at[4], recv_sem.at[1], above)

    for k in chunks:
        place(0, k, choose(k, 2))
    for k in chunks:
        own = choose(k, 0)
        arrived(zgot.at[k], recv_z.at[1, k])
        place(1, k, jnp.where(from_here, own, zgot[k]))

    arrived(wbuf.at[1, pl.ds(1, 3)], recv_sem.at[3])
    wbuf[2, 0] = wbuf[1, 0] + wbuf[1, 1] + wbuf[1, 2] + wbuf[1, 3]
    copy(wbuf.at[2, 0], wbuf.at[2, 1], send_sem.at[7], recv_sem.at[4], across)

    into = lax.broadcasted_iota(jnp.int32, (512, 512), 0)
    out = lax.broadcasted_iota(jnp.int32, (512, 512), 1)
    wanted = ((out // 16) % 4) * 128 + ((out // 64) % 2) * 64 + (out // 128) * 16 + out % 16
    select[...] = jnp.where(into == wanted, 1.0, 0.0).astype(BF16)
    arrived(halo, recv_sem.at[0])
    arrived(field.at[0], recv_sem.at[1])

    has_below = jnp.full((32, 128), (tile > 0).astype(jnp.int32))
    has_above = jnp.full((32, 128), (tile < 15).astype(jnp.int32))

    def inside(i, value):
        if i < HALO:
            return jnp.where(has_below > 0, value, 0.0)
        if i >= HALO + 8:
            return jnp.where(has_above > 0, value, 0.0)
        return value

    for f in range(2):
        for i in (*range(HALO), *range(HALO + 8, 2 * HALO + 8)):
            field[f, i] = inside(i, field[f, i])

    def border(ref, start, width, i):
        if i < HALO:
            return halo[0, start + width - HALO + i]
        if i >= HALO + 8:
            return halo[1, start + i - HALO - 8]
        return ref[i - HALO]

    def sweep(i, v_at):
        here, low, up = v_at(i), v_at(i - 1), v_at(i + 1)
        k = kcon[i]
        kv = k * here
        near = low + up + shifted(here, 0, 0.0) + shifted(here, 1, 0.0)
        weighted = kcon[i - 1] * low + kcon[i + 1] * up + shifted(kv, 0, 0.0) + shifted(kv, 1, 0.0)
        return k, near, weighted, here

    for m in range(2):
        edge = 2 * m
        last = 2 * HALO + 8 - edge
        for i in range(edge, last):
            fresh = border(noise.at[m], 0 if m == 0 else 4, 4 if m == 0 else 2, i)
            value = inside(i, 0.8 * field[0, i] + 0.6 * fresh)
            prop[i] = value
            kcon[i] = jnp.exp(value)
        flag = jnp.full((32, 128), accept[m]) > 0
        for i in range(edge + 1, last - 1):
            k, near, weighted, here = sweep(i, lambda j: field[1, j])
            inv[i] = 0.8 / (6.0 * k + kcon[i - 1] + kcon[i + 1] + shifted(k, 0, 1.0) + shifted(k, 1, 1.0))
            value = 0.2 * here + (2.0 * border(source, 6, 3, i) + k * near + weighted) * inv[i]
            once[i] = inside(i, value)
        if m == 0:
            arrived(field.at[0], send_sem.at[4])
        for i in range(edge + 2, last - 2):
            k, near, weighted, here = sweep(i, lambda j: once[j])
            value = 0.2 * here + (2.0 * border(source, 6, 3, i) + k * near + weighted) * inv[i]
            field[0, i] = jnp.where(flag, prop[i], field[0, i])
            field[1, i] = jnp.where(flag, inside(i, value), field[1, i])

    final = field[1, interior]
    cond_out[...] = field[0, interior]
    pot_out[...] = final

    for d in FAR_FIRST:
        at = pl.ds(HALO + 2 * ((y + d) % 4), 2)
        copy(field.at[1, at], cols.at[0, d], send_sem.at[8], recv_rows.at[0, d], along(1, d))
    cols[0, 0] = field[1, pl.ds(HALO + 2 * y, 2)]
    scaled = final * weights[0]
    stacked = jnp.concatenate(
        [jnp.concatenate([scaled[4 * half + j] for j in range(4)], axis=1) for half in range(2)], axis=0
    )
    high, low = split(stacked)
    shuffled = jnp.dot(high, select[...], preferred_element_type=F32) + jnp.dot(low, select[...], preferred_element_type=F32)
    for j in range(4):
        for half in range(2):
            perm[j, half] = shuffled[32 * half : 32 * half + 32, 128 * j : 128 * j + 128]
    for d in FAR_FIRST:
        copy(perm.at[(x + d) % 4], rows.at[0, d], send_sem.at[9], recv_rows.at[1, d], along(0, d))
    rows[0, 0] = perm[x]

    def forward(src, axis, n):
        for d in FAR_FIRST:
            copy(src.at[0, n], src.at[d, n], send_sem.at[10 + axis], recv_rows.at[axis, 0], along(axis, d))

    forward(cols, 0, 0)
    forward(rows, 1, 0)
    for n in (1, 3, 2):
        arrived(cols.at[0, n], recv_rows.at[0, n])
        forward(cols, 0, n)
        arrived(rows.at[0, n], recv_rows.at[1, n])
        forward(rows, 1, n)
    arrived(cols.at[pl.ds(1, 3)], recv_rows.at[0, 0])
    arrived(rows.at[pl.ds(1, 3)], recv_rows.at[1, 0])

    right = jnp.concatenate(
        [jnp.concatenate([cols[dx, dy, 0], cols[dx, dy, 1]], axis=1) for dy in range(4) for dx in range(4)], axis=0
    )
    right_high, right_low = split(right)
    lefts = [split(jnp.concatenate([rows[dy, dx, half] for dy in range(4) for dx in range(4)], axis=0).T) for half in range(2)]

    parity = z % 2
    beside = z + 1 - 2 * parity
    for h in range(2):
        lanes = slice(128 * h, 128 * h + 128)
        for half in range(2):
            left_high, left_low = lefts[half]
            product = (
                jnp.dot(left_high, right_high[:, lanes], preferred_element_type=F32)
                + jnp.dot(left_high, right_low[:, lanes], preferred_element_type=F32)
                + jnp.dot(left_low, right_high[:, lanes], preferred_element_type=F32)
            )
            for c in range(2):
                for j in range(4):
                    partial[h, c, j % 2, 2 * half + j // 2] = product[64 * c + 16 * j : 64 * c + 16 * j + 16]
        swapped = corner.at[h, pl.ds(0, 2)]
        copy(partial.at[h, 1 - core], swapped, send_sem.at[12], recv_pair.at[0, h], device(x, y, z, 1 - core))
    for h in range(2):
        arrived(corner.at[h, pl.ds(0, 2)], recv_pair.at[0, h])
        both[h] = partial[h, core] + corner[h, 0:2]
        copy(both.at[h, 1 - parity], corner.at[h, 2], send_sem.at[12], recv_pair.at[2, h], device(x, y, beside, core))
    for h in range(2):
        arrived(corner.at[h, 2], recv_pair.at[2, h])
        summed[h] = both[h, parity] + corner[h, 2]
        for d in (8, 6, 10, 4, 12, 2, 14):
            target = device(x, y, (z + d) % 16, core)
            copy(summed.at[h, ((z + d) % 8) // 2], zsum.at[h, d // 2], send_sem.at[13], recv_pair.at[1, h], target)
    arrived(wbuf.at[2, 1], recv_sem.at[4])
    weight_sum = (wbuf[2, 0] + wbuf[2, 1])[0:1, 0:1]
    for h in range(2):
        arrived(zsum.at[h, pl.ds(1, 7)], recv_pair.at[1, h])
        total = summed[h, (z % 8) // 2]
        for d in range(1, 8):
            total = total + zsum[h, d]
        piece = mom_out.at[pl.ds(pl.multiple_of(x * 16, 16), 16), pl.ds(pl.multiple_of(y * 256 + 128 * h, 128), 128)]
        piece[...] = total / weight_sum
        for a in (2, 1, 3, 0):
            for b in (2, 1, 3, 0):
                if a or b:
                    copy(piece, piece, send_sem.at[14], recv_sem.at[7], device((x + a) % 4, (y + b) % 4, z, core))
    many = zsum.at[pl.ds(0, 2), pl.ds(1, 15)]
    arrived(many, recv_sem.at[7])
    three = rows.at[0, pl.ds(1, 3)]
    most = rows.at[pl.ds(1, 3)]
    works = wbuf.at[0, pl.ds(1, 3)]
    likes = (sent, sent, field.at[0], halo, None, works, works, wbuf.at[2, 1], three, three, most, most, corner, zsum.at[pl.ds(0, 2), pl.ds(1, 7)], many)
    for i, like in enumerate(likes):
        if like is not None:
            arrived(like, send_sem.at[i])


def leave(cond, pot, mom, cond_out, pot_out, mom_out, sems):
    copies = [
        pltpu.make_async_copy(src, dst, sems.at[i])
        for i, (src, dst) in enumerate(((mom, mom_out), (cond, cond_out), (pot, pot_out)))
    ]
    for c in copies:
        c.start()
    for c in copies:
        c.wait()


def local(log_cond, potential, noise, source, parents, accept, weights):
    hbm = pl.BlockSpec(memory_space=pl.ANY)
    vmem = pl.BlockSpec(memory_space=pltpu.VMEM)
    dma = pltpu.SemaphoreType.DMA
    block = (8, 32, 128)
    part = (8 // CHUNKS, 32, 128)
    wide = (2 * HALO + 8, 32, 128)
    conduct, pot, moments = pl.pallas_call(
        kernel,
        out_shape=(
            pltpu.VMEM(block, F32),
            pltpu.VMEM(block, F32),
            pltpu.VMEM((64, 1024), F32),
        ),
        in_specs=[hbm] * 4 + [pl.BlockSpec(memory_space=pltpu.HBM)] * 3,
        out_specs=(vmem, vmem, vmem),
        scratch_shapes=[
            (pltpu.VMEM((4, *part), F32),) * CHUNKS,
            (pltpu.VMEM((8, *part), F32),) * CHUNKS,
            pltpu.VMEM((3, CHUNKS, 3, *part), F32),
            ((pltpu.VMEM((4, *part), F32),) * CHUNKS,) * 3,
            pltpu.VMEM((CHUNKS, *part), F32),
            pltpu.VMEM((CHUNKS, *part), F32),
            pltpu.VMEM((2, 9, 32, 128), F32),
            pltpu.VMEM((2, *wide), F32),
            pltpu.VMEM(wide, F32),
            pltpu.VMEM(wide, F32),
            pltpu.VMEM(wide, F32),
            pltpu.VMEM(wide, F32),
            pltpu.SMEM((32,), jnp.int32),
            pltpu.SMEM((2,), jnp.int32),
            pltpu.SMEM((1,), F32),
            pltpu.VMEM((2, *block), F32),
            pltpu.VMEM(block, F32),
            pltpu.VMEM((512, 512), BF16),
            pltpu.VMEM((4, 2, 32, 128), F32),
            pltpu.VMEM((4, 4, 2, 32, 128), F32),
            pltpu.VMEM((4, 4, 2, 32, 128), F32),
            pltpu.VMEM((2, 2, 2, 4, 16, 128), F32),
            pltpu.VMEM((2, 3, 4, 16, 128), F32),
            pltpu.VMEM((2, 2, 4, 16, 128), F32),
            pltpu.VMEM((2, 4, 16, 128), F32),
            pltpu.VMEM((2, 16, 16, 128), F32),
            pltpu.VMEM((3, 4, 8, 128), F32),
            dma((15,)), dma((3, CHUNKS)), dma((3, CHUNKS)), dma((2, CHUNKS)), dma((2, 4)), dma((3, 2)), dma((8,)), dma((6,)),
        ],
        compiler_params=pltpu.CompilerParams(collective_id=0, has_side_effects=True),
        name="resample_move",
    )(log_cond[0], potential[0], noise[:, 0], source, parents, accept.reshape(-1), weights)
    conduct, pot, moments = pl.pallas_call(
        leave,
        out_shape=(
            jax.ShapeDtypeStruct(block, F32),
            jax.ShapeDtypeStruct(block, F32),
            jax.ShapeDtypeStruct((64, 1024), F32),
        ),
        in_specs=[hbm] * 3,
        out_specs=(hbm, hbm, hbm),
        scratch_shapes=[dma((3,))],
        name="leave",
    )(*(pltpu.with_memory_space_constraint(value, pltpu.VMEM) for value in (conduct, pot, moments)))
    return conduct[None], pot[None], moments


def solution(mesh):
    placed = (
        P("grp", "tile", None, None),
        P("grp", "tile", None, None),
        P(None, "grp", "tile", None, None),
        P("tile", None, None),
        P(),
        P(None, "grp"),
        P("grp"),
    )
    return jax.shard_map(
        local,
        mesh=mesh,
        in_specs=placed,
        out_specs=(P("grp", "tile", None, None), P("grp", "tile", None, None), P("tile", None)),
        check_vma=False,
    )
```
